128 devices in a mesh: func: 8 (over z, core), box: 16 (over x, y).
Axes of the slice: x: 4, y: 4, z: 4, core: 2. Of those that a mesh axis runs over, the one named last changes fastest.
Arguments:
- coeffs: bfloat16 [3072, 32, 1024], P(('func', 'box')), may hold values from -8 to 8
- centers: int32 [3072], replicated, may hold values from 0 to 1535, as said below
- kinetic: bfloat16 [1024, 1024], replicated, may hold values from -0.1875 to 0.1875
- potential: float32 [1536, 1024], P(('func', 'box')), may hold values from -1 to 1
Outputs:
- filtered: bfloat16 [3072, 32, 1024], P(('func', 'box'))
- gram_band: float32 [3072, 256], P(('func', 'box'))
The draws below stay inside these ranges and needn't reach their ends.
Inputs may be any that keep to these rules, and one draw needn't show every extreme that they name: `centers`: centers never fall. The boxes form aligned groups of 32, and the groups aligned blocks of four; every box of a group is the center of the same number of functions, 1, 2 or 4, and each block of four groups holds the numbers 1, 1, 2 and 4 in an order whose running total of (number - 2) stays between -1 and 1. So between 32 and 128 functions touch each box, and some box is touched by exactly 128.
All inputs are finite; a program needn't handle non-finite values.
Results may differ from the reference program's by a relative error of at most 0.0057.
Values may be sent and summed in bfloat16 or wider, within the bound.
A program may use at most 64 MiB of HBM per device.

```python
import jax
import jax.numpy as jnp
from jax import lax

SUP = 32
P_SIZE = 1024
NF = 3072
NB = 1536


def draw_coeffs(key, part):
    key_values, key_scales = jax.random.split(key)
    base_values = jnp.clip(jax.random.normal(key_values, (NF, SUP, P_SIZE), jnp.float32), -3.9, 3.9)
    scales = jnp.exp(jax.random.uniform(key_scales, (NF, SUP, 1), jnp.float32, -0.7, 0.7))
    return (base_values * scales).astype(jnp.bfloat16)


def draw_centers(key, part):
    groups = NB // SUP
    blocks = groups // 4
    orders = jnp.array([[1, 2, 4, 1], [1, 4, 1, 2], [1, 4, 2, 1], [2, 1, 4, 1]], dtype=jnp.int32)
    chosen = jax.random.randint(key, (blocks,), 0, 4).astype(jnp.int32)
    density = orders[chosen].reshape(groups)
    counts = jnp.repeat(density, SUP, total_repeat_length=NB)
    box_ends = jnp.cumsum(counts).astype(jnp.int32)
    return jnp.searchsorted(box_ends, jnp.arange(NF, dtype=jnp.int32), side='right').astype(jnp.int32)


def steps_of(own_key, dims, cuts, low, top_value):
    level = 1.0
    for position, blocks in cuts:
        heights = jax.random.uniform(jax.random.fold_in(jax.random.fold_in(own_key, 6), position), (blocks,), jnp.float32, low / len(cuts), top_value / len(cuts))
        level = level * jnp.repeat(jnp.exp(heights), dims[position] // blocks).reshape((-1,) + (1,) * (len(dims) - 1 - position))
    return level


def centred(key, shape, scale, bound, kind=jnp.bfloat16):
    entries = jax.random.normal(key, shape, jnp.float32) * scale
    return jnp.minimum(jnp.maximum(entries, -bound), bound).astype(kind)


def setup_inputs(seed: int = 0) -> dict:
    key_list = jax.random.split(jax.random.key(seed), 5)
    return {
        "coeffs": draw_coeffs(jax.random.fold_in(key_list[4], 71), 0),
        "centers": draw_centers(jax.random.fold_in(key_list[4], 71), 0),
        "kinetic": centred(key_list[2], (P_SIZE, P_SIZE), P_SIZE ** -0.5, 0.1875),
        "potential": jnp.clip(jax.random.uniform(key_list[3], (NB, P_SIZE), jnp.float32, -1.0, 1.0) * steps_of(key_list[3], (NB, P_SIZE), ((0, 128),), -0.4, 0.0), -1.0, 1.0),
    }


group_boxes = 16


def to_band(matrix):
    leading = matrix.shape[:-2]
    matrix_order = matrix.shape[-1]
    spaces = [(0, 0)] * len(leading)
    padded = jnp.pad(matrix, spaces + [(0, 0), (matrix_order - 1, 1)])
    flattened = padded.reshape(leading + (2 * matrix_order * matrix_order,))
    flattened = jnp.pad(flattened, spaces + [(0, matrix_order)])
    return flattened.reshape(leading + (matrix_order, 2 * matrix_order + 1))[..., : 2 * matrix_order]


def from_band(band_rows):
    leading = band_rows.shape[:-2]
    matrix_order = band_rows.shape[-2]
    flattened = band_rows.reshape(leading + (2 * matrix_order * matrix_order,))
    flattened = flattened[..., : matrix_order * (2 * matrix_order - 1)]
    return flattened.reshape(leading + (matrix_order, 2 * matrix_order - 1))[..., matrix_order - 1:]


def reference(coeffs, centers, kinetic, potential):
    capacity = 4 * SUP
    volume = 1.0 / (SUP * P_SIZE)
    every_box = jnp.arange(NB, dtype=jnp.int32)
    window_start = (every_box - SUP + 1) % NB
    first_row = jnp.searchsorted(centers, window_start, side="left").astype(jnp.int32)
    end_row = jnp.searchsorted(centers, every_box + 1, side="left").astype(jnp.int32)
    filled = (end_row - first_row) % NF
    flat_coeffs = coeffs.reshape(NF * SUP, P_SIZE)
    potential_all = potential.reshape(NB, P_SIZE)
    slot_ids = jnp.arange(capacity, dtype=jnp.int32)

    def gather_box(first_box):
        box_ids = first_box + jnp.arange(group_boxes, dtype=jnp.int32)
        row_ids = (first_row[box_ids][:, None] + slot_ids[None, :]) % NF
        live_slot = slot_ids[None, :] < filled[box_ids][:, None]
        support_step = jnp.minimum((box_ids[:, None] - centers[row_ids]) % NB, SUP - 1)
        target = (row_ids * SUP + support_step).astype(jnp.int32)
        pieces = jnp.where(live_slot[..., None], flat_coeffs[target], jnp.zeros((), coeffs.dtype))
        return box_ids, row_ids, live_slot, target, pieces

    def first_pass(running, first_box):
        box_ids, row_ids, live_slot, target, pieces = gather_box(first_box)
        widened = pieces.astype(jnp.float32)
        gram_box = volume * jnp.einsum("kmp,knp->kmn", widened, widened)
        band_rows = to_band(gram_box)
        running = running.at[row_ids.reshape(-1)].add(band_rows.reshape(-1, 2 * capacity))
        return running, None

    starts = jnp.arange(NB // group_boxes, dtype=jnp.int32) * group_boxes
    gram_band, unused = lax.scan(first_pass, jnp.zeros((NF, 2 * capacity), jnp.float32), starts)
    diag_mask = (jnp.arange(2 * capacity) == capacity - 1).astype(jnp.float32)
    correction = (1.5 * diag_mask - 0.5 * gram_band).astype(jnp.bfloat16)

    def second_pass(running, first_box):
        box_ids, row_ids, live_slot, target, pieces = gather_box(first_box)
        mixing = from_band(correction[row_ids])
        corrected = jnp.einsum("kml,klp->kmp", mixing.astype(jnp.float32), pieces.astype(jnp.float32)).astype(jnp.bfloat16)
        widened = corrected.astype(jnp.float32)
        applied = jnp.einsum("kmp,pq->kmq", widened, kinetic.astype(jnp.float32))
        applied = (applied + potential_all[box_ids][:, None, :] * widened).astype(jnp.bfloat16)
        placing = jnp.where(live_slot, target, NF * SUP).astype(jnp.int32)
        running = running.at[placing.reshape(-1)].set(applied.reshape(-1, P_SIZE), mode="drop")
        return running, None

    filtered, unused = lax.scan(second_pass, jnp.zeros((NF * SUP, P_SIZE), jnp.bfloat16), starts)
    return filtered.reshape(NF, SUP, P_SIZE), gram_band
```

```python
import jax
import jax.numpy as jnp
from jax import lax
from jax.experimental import pallas as pl
from jax.experimental.pallas import tpu as pltpu
from jax.sharding import PartitionSpec as P

MESH = pl.DeviceIdType.MESH
BF = jnp.bfloat16
F32 = jnp.float32

SUP = 32
FUN = 24
BOX = 12
RING = 4
OWN = FUN * RING
FRAME = 256
LEFT = 80
SLICE = 256
REACH = 7
BOX_ALL = 1536
FUN_ALL = 3072
VOLUME = 1.0 / (32 * 1024)

FORWARD = (
    (80, 0, 2, 176, -1),
    (144, 2, 2, 48, 1),
    (112, 0, 1, 208, -1),
    (112, 3, 1, 16, 1),
)
NEEDS = (
    ((0, 0), (0, 1), (1, 0), (1, 1)),
    ((3, 3), (3, 2), (2, 3), (2, 2)),
    ((1, 0), (2, 0)),
    ((2, 3), (1, 3)),
)


def exchange_kernel(
    coeffs, pot, meta, y_out, v_out, gram_out,
    frame, slots, back_a, back_b, back_c, back_d, gram, terms, sums, rows_out, rows_in, mixing, potb, boxes,
    y_send, y_recv, x_send, x_recv, v_send, v_recv, s_send, s_recv, c_send, c_recv, bx_send, bx_recv, by_send, by_recv,
):
    me = lax.axis_index("func") * 16 + lax.axis_index("box")
    y = lax.rem(me, RING)
    base = me - y

    def dev(linear):
        wrapped = lax.rem(linear + 128, 128)
        return (lax.div(wrapped, 16), lax.rem(wrapped, 16))

    barrier = pltpu.get_barrier_semaphore()
    for k in range(1, REACH + 1):
        for sign in (1, -1):
            pl.semaphore_signal(barrier, inc=1, device_id=dev(me + sign * k), device_id_type=MESH)

    frame[16:48, 0:3] = jnp.zeros((32, 3, 8, SLICE), BF)
    frame[48:80, 0:2] = jnp.zeros((32, 2, 8, SLICE), BF)
    frame[176:208, 2:4] = jnp.zeros((32, 2, 8, SLICE), BF)
    frame[208:240, 1:4] = jnp.zeros((32, 3, 8, SLICE), BF)
    slots[:, 0:16, :] = jnp.zeros((SUP, 16, SLICE), BF)
    slots[:, 240:256, :] = jnp.zeros((SUP, 16, SLICE), BF)
    potb[0:BOX, :] = pot[...].astype(BF)
    potb[BOX:16, :] = jnp.zeros((16 - BOX, 1024), BF)
    pl.semaphore_wait(barrier, 2 * REACH)

    started = []

    my_rows = pl.ds(pl.multiple_of(LEFT + FUN * y, 8), FUN)
    high = lax.div(y, 2)
    for p in range(4):
        q0 = (0, 1, 3, 2)[p]
        q = q0 + high * (3 - 2 * q0)
        for k in (1, 3, 2):
            yp = lax.rem(y + k, RING)
            copy = pltpu.make_async_remote_copy(
                src_ref=coeffs.at[:, q, :, pl.ds(pl.multiple_of(yp * SLICE, SLICE), SLICE)],
                dst_ref=frame.at[my_rows, q],
                send_sem=y_send.at[k - 1, p],
                recv_sem=y_recv.at[y, q],
                device_id=dev(base + yp),
                device_id_type=MESH,
            )
            copy.start()
            started.append(copy)
        pltpu.make_async_copy(
            coeffs.at[:, q, :, pl.ds(pl.multiple_of(y * SLICE, SLICE), SLICE)],
            frame.at[my_rows, q],
            y_recv.at[y, q],
        ).start()

    v_copies = []
    for o in range(-2, 5):
        if o == 0:
            copy = pltpu.make_async_copy(potb, v_out.at[2], v_recv.at[2])
        else:
            copy = pltpu.make_async_remote_copy(
                src_ref=potb,
                dst_ref=v_out.at[o + 2],
                send_sem=v_send.at[o + 2],
                recv_sem=v_recv.at[o + 2],
                device_id=dev(me - o),
                device_id_type=MESH,
            )
        copy.start()
        v_copies.append(copy)

    arrived = set()

    def wait_piece(ys, q):
        if (ys, q) in arrived:
            return
        arrived.add((ys, q))
        piece = frame.at[pl.ds(LEFT + FUN * ys, FUN), q]
        pltpu.make_async_copy(piece, piece, y_recv.at[ys, q]).wait()

    forwards = []
    for n, (src, q, nq, dst, to) in enumerate(FORWARD):
        for ys, quarter in NEEDS[n]:
            wait_piece(ys, quarter)
        copy = pltpu.make_async_remote_copy(
            src_ref=frame.at[pl.ds(src, 32), pl.ds(q, nq)],
            dst_ref=frame.at[pl.ds(dst, 32), pl.ds(q, nq)],
            send_sem=x_send.at[n],
            recv_sem=x_recv.at[n],
            device_id=dev(me + RING * to),
            device_id_type=MESH,
        )
        copy.start()
        forwards.append(copy)
    for ys in range(RING):
        for q in range(4):
            wait_piece(ys, q)

    row_id = lax.broadcasted_iota(jnp.int32, (FRAME, FRAME), 0)
    col_id = lax.broadcasted_iota(jnp.int32, (FRAME, FRAME), 1)

    def into_slots(pair, carry):
        parts = []
        for half in range(2):
            octet = 2 * pair + half
            select = (row_id == meta[pl.ds(8 + octet, 1), :]).astype(F32).astype(BF)
            raw = frame[pl.ds(pl.multiple_of(8 * octet, 8), 8)]
            raw = raw.astype(F32).reshape(FRAME, SLICE).astype(BF)
            out = jnp.dot(select, raw, preferred_element_type=F32)
            parts.append(out.reshape(SUP, 8, SLICE))
        both = jnp.concatenate(parts, axis=1).astype(BF)
        slots[:, pl.ds(pl.multiple_of(16 * pair, 16), 16), :] = both
        return carry

    lax.fori_loop(5, 11, into_slots, 0)
    for copy in forwards:
        copy.wait_recv()
    lax.fori_loop(1, 5, into_slots, 0)
    lax.fori_loop(11, 15, into_slots, 0)

    rel_row = meta[0:1, :]
    rel_tile = jnp.broadcast_to(rel_row, (FRAME, FRAME))
    rel_col = jnp.sum(
        jnp.where(row_id == col_id, rel_tile.astype(F32), 0.0), axis=1, keepdims=True
    ).astype(jnp.int32)
    low_row = meta[1:2, :]
    top_row = meta[2:3, :]
    boxes[...] = jnp.broadcast_to(rel_col, (FRAME, FRAME))

    def same_box(slot):
        box_row = rel_row + jnp.bitwise_and(slot - rel_row, SUP - 1)
        owned = jnp.logical_and(box_row >= low_row, box_row <= top_row)
        box_row = jnp.where(owned, box_row, -1)
        col = boxes[...]
        box_col = col + jnp.bitwise_and(slot - col, SUP - 1)
        return box_col == box_row

    gram[...] = jnp.zeros((FRAME, FRAME), F32)

    def gram_step(slot, carry):
        held = slots[slot]
        prod = lax.dot_general(held, held, (((1,), (1,)), ((), ())), preferred_element_type=F32)
        gram[...] += jnp.where(same_box(slot), prod, 0.0)
        return carry

    lax.fori_loop(0, SUP, gram_step, 0)
    gram[...] = gram[...] * VOLUME

    s_copies = []

    def send_terms(n, start, slot, target):
        copy = pltpu.make_async_remote_copy(
            src_ref=gram.at[pl.ds(start, FUN)],
            dst_ref=terms.at[slot],
            send_sem=s_send.at[n],
            recv_sem=s_recv.at[slot],
            device_id=dev(target),
            device_id_type=MESH,
        )
        copy.start()
        s_copies.append(copy)

    for k in range(1, 4):
        yp = lax.rem(y + k, RING)
        send_terms(k - 1, pl.multiple_of(LEFT + FUN * yp, 8), 4 + y, base + yp)
    for yp in range(1, 4):
        send_terms(2 + yp, FUN * yp - 16, 8 + y, base - RING + yp)
    for yp in range(0, 3):
        send_terms(6 + yp, 176 + FUN * yp, y, base + RING + yp)

    def wait_terms(slot):
        pltpu.make_async_copy(terms.at[slot], terms.at[slot], s_recv.at[slot]).wait()

    sums[0] = jnp.zeros((FUN, FRAME), F32)
    sums[2] = jnp.zeros((FUN, FRAME), F32)
    sums[1] = gram[my_rows, :]
    for k in range(1, 4):
        slot = 4 + lax.rem(y + k, RING)
        wait_terms(slot)
        sums[1] += terms[slot]

    @pl.when(y <= 2)
    def _():
        for ys in range(RING):
            wait_terms(ys)
        sums[0] = terms[0] + terms[1] + terms[2] + terms[3]

    @pl.when(y >= 1)
    def _():
        for ys in range(RING):
            wait_terms(8 + ys)
        sums[2] = terms[8] + terms[9] + terms[10] + terms[11]

    pad = jnp.zeros((FUN, FRAME), F32)
    wide = jnp.concatenate([sums[0], pad], axis=1)
    wide += pltpu.roll(jnp.concatenate([sums[1], pad], axis=1), 96, 1)
    wide += pltpu.roll(jnp.concatenate([sums[2], pad], axis=1), 192, 1)
    lane = lax.broadcasted_iota(jnp.int32, (FUN, 512), 1)
    sub = lax.broadcasted_iota(jnp.int32, (FUN, 512), 0)
    fixed = (1.5 * (lane == sub + (FUN * y + 176)).astype(F32) - 0.5 * wide)
    rows_out[0] = fixed[:, 0:256].astype(BF)
    rows_out[1] = pltpu.roll(fixed, 512 - 96, 1)[:, 0:256].astype(BF)
    rows_out[2] = pltpu.roll(fixed, 512 - 192, 1)[:, 0:256].astype(BF)

    c_copies = []

    def send_rows(n, which, slot, target):
        copy = pltpu.make_async_remote_copy(
            src_ref=rows_out.at[which],
            dst_ref=rows_in.at[slot],
            send_sem=c_send.at[n],
            recv_sem=c_recv.at[slot],
            device_id=dev(target),
            device_id_type=MESH,
        )
        copy.start()
        return copy

    own_rows = [
        send_rows(k - 1, 1, 4 + y, base + lax.rem(y + k, RING)) for k in range(1, 4)
    ]

    @pl.when(y <= 2)
    def _():
        for yp in range(RING):
            send_rows(3 + yp, 0, 8 + y, base - RING + yp)

    @pl.when(y >= 1)
    def _():
        for yp in range(RING):
            send_rows(7 + yp, 2, y, base + RING + yp)

    band = pltpu.roll(wide, 512 - 49 - FUN * y, 1)
    for bit in range(5):
        moved = pltpu.roll(band, 512 - (1 << bit), 1)
        band = jnp.where(jnp.bitwise_and(sub, 1 << bit) != 0, moved, band)
    gram_out[...] = jnp.where(lane[:, 0:256] == 255, 0.0, band[:, 0:256])

    def wait_rows(slot):
        pltpu.make_async_copy(rows_in.at[slot], rows_in.at[slot], c_recv.at[slot]).wait()

    mixing[0:16, :] = jnp.zeros((16, FRAME), F32)
    mixing[240:256, :] = jnp.zeros((16, FRAME), F32)
    mixing[my_rows, :] = rows_out[1].astype(F32)
    for k in range(1, 4):
        ys = lax.rem(y + k, RING)
        wait_rows(4 + ys)
        mixing[pl.ds(pl.multiple_of(LEFT + FUN * ys, 8), FUN), :] = rows_in[4 + ys].astype(F32)
    for ys in range(0, 3):
        wait_rows(8 + ys)
        mixing[176 + FUN * ys : 200 + FUN * ys, :] = rows_in[8 + ys].astype(F32)
    for ys in range(1, 4):
        wait_rows(ys)
        mixing[FUN * ys - 16 : FUN * ys + 8, :] = rows_in[ys].astype(F32)

    def mix_step(slot, carry):
        mix = jnp.where(same_box(slot), mixing[...], 0.0).astype(BF)
        slots[slot] = jnp.dot(mix, slots[slot], preferred_element_type=F32).astype(BF)
        return carry

    lax.fori_loop(0, SUP, mix_step, 0)

    for copy in forwards:
        copy.wait_send()

    def out_of_slots(pair, carry):
        both = slots[:, pl.ds(pl.multiple_of(16 * pair, 16), 16), :].astype(F32)
        for half in range(2):
            octet = 2 * pair + half
            select = (row_id == meta[pl.ds(40 + octet, 1), :]).astype(F32).astype(BF)
            part = both[:, 8 * half : 8 * half + 8, :].reshape(FRAME, SLICE).astype(BF)
            out = jnp.dot(select, part, preferred_element_type=F32)
            frame[pl.ds(pl.multiple_of(8 * octet, 8), 8)] = out.reshape(8, 4, 8, SLICE).astype(BF)
        return carry

    lax.fori_loop(1, 5, out_of_slots, 0)
    lax.fori_loop(11, 15, out_of_slots, 0)
    backs = (back_a, back_b, back_c, back_d)
    x_backs = []
    for n, (src, q, nq, dst, to) in enumerate(FORWARD):
        copy = pltpu.make_async_remote_copy(
            src_ref=frame.at[pl.ds(dst, 32), pl.ds(q, nq)],
            dst_ref=backs[n],
            send_sem=bx_send.at[n],
            recv_sem=bx_recv.at[n],
            device_id=dev(me - RING * to),
            device_id_type=MESH,
        )
        copy.start()
        x_backs.append(copy)
    lax.fori_loop(5, 11, out_of_slots, 0)
    for n, (src, q, nq, dst, to) in enumerate(FORWARD):
        x_backs[n].wait_recv()
        mine = frame[src : src + 32, q : q + nq].astype(F32)
        frame[src : src + 32, q : q + nq] = (mine + backs[n][...].astype(F32)).astype(BF)

    lanes = pl.ds(pl.multiple_of(y * SLICE, SLICE), SLICE)
    y_backs = []
    for k in (1, 3, 2):
        yp = lax.rem(y + k, RING)
        copy = pltpu.make_async_remote_copy(
            src_ref=frame.at[pl.ds(pl.multiple_of(LEFT + FUN * yp, 8), FUN)],
            dst_ref=y_out.at[:, :, :, lanes],
            send_sem=by_send.at[k - 1],
            recv_sem=by_recv.at[y],
            device_id=dev(base + yp),
            device_id_type=MESH,
        )
        copy.start()
        y_backs.append(copy)
    home = pltpu.make_async_copy(frame.at[my_rows], y_out.at[:, :, :, lanes], by_recv.at[y])
    home.start()

    for copy in started:
        copy.wait_send()
    for copy in v_copies:
        copy.wait()
    for copy in s_copies:
        copy.wait_send()
    for copy in own_rows:
        copy.wait_send()

    @pl.when(y <= 2)
    def _():
        for yp in range(RING):
            pltpu.make_async_copy(rows_out.at[0], rows_out.at[0], c_send.at[3 + yp]).wait()

    @pl.when(y >= 1)
    def _():
        for yp in range(RING):
            pltpu.make_async_copy(rows_out.at[2], rows_out.at[2], c_send.at[7 + yp]).wait()

    for copy in x_backs:
        copy.wait_send()
    for copy in y_backs:
        copy.wait_send()
    for ys in range(RING):
        part = y_out.at[:, :, :, pl.ds(ys * SLICE, SLICE)]
        pltpu.make_async_copy(part, part, by_recv.at[ys]).wait()


def filter_kernel(starts, pieces, kinetic, pot, out, pot_rows):
    step = pl.program_id(0)

    @pl.when(step == 0)
    def _():
        for k in range(7):
            pot_rows[BOX * k : BOX * k + BOX, :] = pot[k].astype(F32)[0:BOX]

    held = pieces[...]
    applied = jnp.dot(held, kinetic[...], preferred_element_type=F32)
    for j in range(8):
        rows = slice(SUP * j, SUP * j + SUP)
        start = starts[8 * step + j]
        rest = lax.rem(start, 8)
        local = pot_rows[pl.ds(pl.multiple_of(start - rest, 8), SUP + 8), :]
        local = pltpu.roll(local, lax.rem(SUP + 8 - rest, SUP + 8), 0)[0:SUP]
        out[rows, :] = (applied[rows] + local * held[rows].astype(F32)).astype(BF)


def on_device(coeffs, centers, kinetic, potential):
    me = lax.axis_index("func") * 16 + lax.axis_index("box")
    ring = me // RING
    around = jnp.concatenate([centers[-LEFT:], centers, centers[: FRAME - LEFT]])
    near = lax.dynamic_slice_in_dim(around, ring * OWN, FRAME)
    first = near[LEFT]
    rel = (near - first + OWN) % BOX_ALL
    octets = rel.reshape(32, 8)
    eight = jnp.arange(8, dtype=jnp.int32)
    steps = jnp.arange(SUP, dtype=jnp.int32)
    into = ((octets[:, :, None] + steps[None, None, :]) % SUP) * 8 + eight[None, :, None]
    outof = eight[None, None, :] * SUP + (steps[None, :, None] - octets[:, None, :]) % SUP
    low = jnp.broadcast_to(rel[LEFT] + 16, (1, FRAME))
    top = jnp.broadcast_to(rel[LEFT + OWN - 1] + 16, (1, FRAME))
    meta = jnp.concatenate(
        [
            rel.reshape(1, FRAME),
            low,
            top,
            jnp.zeros((5, FRAME), jnp.int32),
            into.reshape(32, FRAME),
            outof.reshape(32, FRAME),
        ]
    )
    my_centers = lax.dynamic_slice_in_dim(centers, me * FUN, FUN)
    starts = (my_centers - BOX * (me - 2)) % BOX_ALL

    hbm = pl.BlockSpec(memory_space=pl.ANY)
    vmem = pl.BlockSpec(memory_space=pltpu.VMEM)
    dma = pltpu.SemaphoreType.DMA
    pieces, pot, gram_band = pl.pallas_call(
        exchange_kernel,
        out_shape=(
            jax.ShapeDtypeStruct((FUN, 4, 8, 1024), BF),
            jax.ShapeDtypeStruct((7, 16, 1024), BF),
            jax.ShapeDtypeStruct((FUN, FRAME), F32),
        ),
        in_specs=[hbm, vmem, vmem],
        out_specs=(hbm, hbm, vmem),
        scratch_shapes=[
            pltpu.VMEM((FRAME, 4, 8, SLICE), BF),
            pltpu.VMEM((SUP, FRAME, SLICE), BF),
            pltpu.VMEM((32, 2, 8, SLICE), BF),
            pltpu.VMEM((32, 2, 8, SLICE), BF),
            pltpu.VMEM((32, 1, 8, SLICE), BF),
            pltpu.VMEM((32, 1, 8, SLICE), BF),
            pltpu.VMEM((FRAME, FRAME), F32),
            pltpu.VMEM((12, FUN, FRAME), F32),
            pltpu.VMEM((3, FUN, FRAME), F32),
            pltpu.VMEM((3, FUN, FRAME), BF),
            pltpu.VMEM((12, FUN, FRAME), BF),
            pltpu.VMEM((FRAME, FRAME), F32),
            pltpu.VMEM((16, 1024), BF),
            pltpu.VMEM((FRAME, FRAME), jnp.int32),
            dma((3, 4)), dma((4, 4)), dma((4,)), dma((4,)), dma((7,)), dma((7,)),
            dma((9,)), dma((12,)), dma((11,)), dma((12,)), dma((4,)), dma((4,)), dma((3,)), dma((4,)),
        ],
        compiler_params=pltpu.CompilerParams(collective_id=0, has_side_effects=True),
        name="exchange",
    )(coeffs.reshape(FUN, 4, 8, 1024), potential, meta)

    filtered = pl.pallas_call(
        filter_kernel,
        grid_spec=pltpu.PrefetchScalarGridSpec(
            num_scalar_prefetch=1,
            grid=(3,),
            in_specs=[
                pl.BlockSpec((256, 1024), lambda i, s: (i, 0)),
                pl.BlockSpec((1024, 1024), lambda i, s: (0, 0)),
                pl.BlockSpec((7, 16, 1024), lambda i, s: (0, 0, 0)),
            ],
            out_specs=pl.BlockSpec((256, 1024), lambda i, s: (i, 0)),
            scratch_shapes=[pltpu.VMEM((128, 1024), F32)],
        ),
        out_shape=jax.ShapeDtypeStruct((FUN * SUP, 1024), BF),
        name="filter",
    )(starts, pieces.reshape(FUN * SUP, 1024), kinetic, pot)
    return filtered.reshape(FUN, SUP, 1024), gram_band


def solution(mesh):
    placed = (P(("func", "box"), None, None), P(), P(), P(("func", "box"), None))
    return jax.shard_map(
        on_device,
        mesh=mesh,
        in_specs=placed,
        out_specs=(P(("func", "box"), None, None), P(("func", "box"), None)),
        check_vma=False,
    )
```

```python
import jax
import jax.numpy as jnp
from jax import lax
from jax.experimental import pallas as pl
from jax.experimental.pallas import tpu as pltpu
from jax.sharding import PartitionSpec as P

MESH = pl.DeviceIdType.MESH
BF = jnp.bfloat16
F32 = jnp.float32

SUP = 32
FUN = 24
BOX = 12
RING = 4
OWN = FUN * RING
FRAME = 256
LEFT = 80
SLICE = 256
REACH = 7
BOX_ALL = 1536
FUN_ALL = 3072
VOLUME = 1.0 / (32 * 1024)

FORWARD = (
    (80, 0, 2, 176, -1),
    (144, 2, 2, 48, 1),
    (112, 0, 1, 208, -1),
    (112, 3, 1, 16, 1),
)
NEEDS = (
    ((0, 0), (0, 1), (1, 0), (1, 1)),
    ((3, 3), (3, 2), (2, 3), (2, 2)),
    ((1, 0), (2, 0)),
    ((2, 3), (1, 3)),
)


def exchange_kernel(
    coeffs, kinetic, pot, lanes_in, out, gram_out,
    frame, slots, back_a, back_b, back_c, back_d, gram, terms, sums, rows_out, rows_in, mixing, potb, boxes,
    meta, starts, kin, v_win, pot_rows, pot_own, y_in, x_in, y_res,
    y_send, y_recv, x_send, x_recv, v_send, v_recv, s_send, s_recv, c_send, c_recv, bx_send, bx_recv,
    by_send, by_recv, kin_sem, out_sem,
):
    me = lax.axis_index("func") * 16 + lax.axis_index("box")
    y = lax.rem(me, RING)
    base = me - y

    def dev(linear):
        wrapped = lax.rem(linear + 128, 128)
        return (lax.div(wrapped, 16), lax.rem(wrapped, 16))

    barrier = pltpu.get_barrier_semaphore()
    for k in range(1, REACH + 1):
        for sign in (1, -1):
            pl.semaphore_signal(barrier, inc=1, device_id=dev(me + sign * k), device_id_type=MESH)

    kin_copy = pltpu.make_async_copy(kinetic, kin, kin_sem)
    kin_copy.start()

    frame[16:48, 0:3] = jnp.zeros((32, 3, 8, SLICE), BF)
    frame[48:80, 0:2] = jnp.zeros((32, 2, 8, SLICE), BF)
    frame[176:208, 2:4] = jnp.zeros((32, 2, 8, SLICE), BF)
    frame[208:240, 1:4] = jnp.zeros((32, 3, 8, SLICE), BF)
    slots[:, 0:16, :] = jnp.zeros((SUP, 16, SLICE), BF)
    slots[:, 240:256, :] = jnp.zeros((SUP, 16, SLICE), BF)
    potb[0:BOX, :] = pot[...].astype(BF)
    potb[BOX:16, :] = jnp.zeros((16 - BOX, 1024), BF)
    pl.semaphore_wait(barrier, 2 * REACH)

    started = []

    my_rows = pl.ds(pl.multiple_of(LEFT + FUN * y, 8), FUN)
    high = lax.div(y, 2)
    for p in range(4):
        q0 = (0, 1, 3, 2)[p]
        q = q0 + high * (3 - 2 * q0)
        for k in (1, 3, 2):
            yp = lax.rem(y + k, RING)
            copy = pltpu.make_async_remote_copy(
                src_ref=coeffs.at[:, q, :, pl.ds(pl.multiple_of(yp * SLICE, SLICE), SLICE)],
                dst_ref=frame.at[my_rows, q],
                send_sem=y_send.at[k - 1, p],
                recv_sem=y_recv.at[y, q],
                device_id=dev(base + yp),
                device_id_type=MESH,
            )
            copy.start()
            started.append(copy)
        pltpu.make_async_copy(
            coeffs.at[:, q, :, pl.ds(pl.multiple_of(y * SLICE, SLICE), SLICE)],
            frame.at[my_rows, q],
            y_recv.at[y, q],
        ).start()

    v_copies = []
    for o in range(-2, 5):
        if o == 0:
            copy = pltpu.make_async_copy(potb, v_win.at[2], v_recv.at[2])
        else:
            copy = pltpu.make_async_remote_copy(
                src_ref=potb,
                dst_ref=v_win.at[o + 2],
                send_sem=v_send.at[o + 2],
                recv_sem=v_recv.at[o + 2],
                device_id=dev(me - o),
                device_id_type=MESH,
            )
        copy.start()
        v_copies.append(copy)

    ring = lax.div(me, RING)
    flat = ring * OWN - LEFT + FUN_ALL
    top_line = lax.div(flat, 128)
    lines = [lanes_in[pl.ds(lax.rem(top_line + k, FUN_ALL // 128), 1), :] for k in range(3)]
    near = pltpu.roll(jnp.concatenate(lines, axis=1), 384 - lax.rem(flat, 128), 1)[:, 0:FRAME]
    row_lane = lax.broadcasted_iota(jnp.int32, (1, FRAME), 1)

    def pick(row, lane_at):
        return jnp.sum(jnp.where(row_lane == lane_at, row, 0), axis=1, keepdims=True)

    rel_row = near - pick(near, LEFT) + OWN
    rel_row = jnp.where(rel_row < 0, rel_row + BOX_ALL, rel_row)
    rel_row = jnp.where(rel_row >= BOX_ALL, rel_row - BOX_ALL, rel_row)
    low_row = OWN + 16
    top_row = pick(rel_row, LEFT + OWN - 1) + 16
    row_id = lax.broadcasted_iota(jnp.int32, (FRAME, FRAME), 0)
    col_id = lax.broadcasted_iota(jnp.int32, (FRAME, FRAME), 1)
    rel_tile = jnp.broadcast_to(rel_row, (FRAME, FRAME))
    rel_col = jnp.sum(
        jnp.where(row_id == col_id, rel_tile.astype(F32), 0.0), axis=1, keepdims=True
    ).astype(jnp.int32)
    boxes[...] = jnp.broadcast_to(rel_col, (FRAME, 128))
    sub_o = lax.broadcasted_iota(jnp.int32, (32, FRAME), 0)
    lane_o = lax.broadcasted_iota(jnp.int32, (32, FRAME), 1)
    rest_row = jnp.bitwise_and(rel_row, SUP - 1)
    spread = jnp.where(
        lax.shift_right_logical(lane_o, 3) == sub_o, jnp.broadcast_to(rest_row, (32, FRAME)), 0
    ).astype(F32).astype(BF)
    in_octet = jnp.bitwise_and(row_id, 7)
    by_fun = (in_octet == lax.shift_right_logical(col_id, 5)).astype(F32).astype(BF)
    by_low = (in_octet == jnp.bitwise_and(col_id, 7)).astype(F32).astype(BF)
    rest_fun = jnp.dot(spread, by_fun, preferred_element_type=F32).astype(jnp.int32)
    rest_low = jnp.dot(spread, by_low, preferred_element_type=F32).astype(jnp.int32)
    meta[0:32, :] = jnp.bitwise_and(rest_fun + lane_o, SUP - 1) * 8 + lax.shift_right_logical(lane_o, 5)
    meta[32:64, :] = jnp.bitwise_and(lane_o, 7) * SUP + jnp.bitwise_and(
        lax.shift_right_logical(lane_o, 3) - rest_low, SUP - 1
    )

    start_row = near - BOX * (me - 2)
    start_row = jnp.where(start_row < 0, start_row + BOX_ALL, start_row)
    start_row = jnp.where(start_row >= BOX_ALL, start_row - BOX_ALL, start_row)
    start_row = jnp.minimum(start_row, 127)
    spread = jnp.where(
        lax.shift_right_logical(lane_o, 3) == sub_o, jnp.broadcast_to(start_row, (32, FRAME)), 0
    ).astype(F32).astype(BF)
    starts[...] = jnp.dot(spread, by_fun, preferred_element_type=F32).astype(jnp.int32) + jnp.bitwise_and(
        lane_o, SUP - 1
    )

    arrived = set()

    def wait_piece(ys, q):
        if (ys, q) in arrived:
            return
        arrived.add((ys, q))
        piece = frame.at[pl.ds(LEFT + FUN * ys, FUN), q]
        pltpu.make_async_copy(piece, piece, y_recv.at[ys, q]).wait()

    forwards = []
    for n, (src, q, nq, dst, to) in enumerate(FORWARD):
        for ys, quarter in NEEDS[n]:
            wait_piece(ys, quarter)
        copy = pltpu.make_async_remote_copy(
            src_ref=frame.at[pl.ds(src, 32), pl.ds(q, nq)],
            dst_ref=frame.at[pl.ds(dst, 32), pl.ds(q, nq)],
            send_sem=x_send.at[n],
            recv_sem=x_recv.at[n],
            device_id=dev(me + RING * to),
            device_id_type=MESH,
        )
        copy.start()
        forwards.append(copy)
    for ys in range(RING):
        for q in range(4):
            wait_piece(ys, q)

    def into_slots(pair, carry):
        parts = []
        for half in range(2):
            octet = 2 * pair + half
            select = (row_id == meta[pl.ds(octet, 1), :]).astype(F32).astype(BF)
            raw = frame[pl.ds(pl.multiple_of(8 * octet, 8), 8)]
            raw = raw.astype(F32).reshape(FRAME, SLICE).astype(BF)
            out = jnp.dot(select, raw, preferred_element_type=F32)
            parts.append(out.reshape(SUP, 8, SLICE))
        both = jnp.concatenate(parts, axis=1).astype(BF)
        slots[:, pl.ds(pl.multiple_of(16 * pair, 16), 16), :] = both
        return carry

    lax.fori_loop(5, 11, into_slots, 0)
    for copy in forwards:
        copy.wait_recv()
    lax.fori_loop(1, 5, into_slots, 0)
    lax.fori_loop(11, 15, into_slots, 0)

    def same_box(slot):
        box_row = rel_row + jnp.bitwise_and(slot - rel_row, SUP - 1)
        owned = jnp.logical_and(box_row >= low_row, box_row <= top_row)
        box_row = jnp.where(owned, box_row, -1)
        col = boxes[...]
        box_col = col + jnp.bitwise_and(slot - col, SUP - 1)
        return box_col == box_row[:, 0:128], box_col == box_row[:, 128:256]

    gram[...] = jnp.zeros((FRAME, FRAME), F32)

    def gram_step(step, carry):
        lo, hi = gram[:, 0:128], gram[:, 128:256]
        for part in range(4):
            slot = 4 * step + part
            held = slots[slot]
            prod = lax.dot_general(held, held, (((1,), (1,)), ((), ())), preferred_element_type=F32)
            same_lo, same_hi = same_box(slot)
            lo = lo + jnp.where(same_lo, prod[:, 0:128], 0.0)
            hi = hi + jnp.where(same_hi, prod[:, 128:256], 0.0)
        gram[:, 0:128] = lo
        gram[:, 128:256] = hi
        return carry

    lax.fori_loop(0, SUP // 4, gram_step, 0)
    gram[...] = gram[...] * VOLUME

    s_copies = []

    def send_terms(n, start, slot, target):
        copy = pltpu.make_async_remote_copy(
            src_ref=gram.at[pl.ds(start, FUN)],
            dst_ref=terms.at[slot],
            send_sem=s_send.at[n],
            recv_sem=s_recv.at[slot],
            device_id=dev(target),
            device_id_type=MESH,
        )
        copy.start()
        s_copies.append(copy)

    for k in range(1, 4):
        yp = lax.rem(y + k, RING)
        send_terms(k - 1, pl.multiple_of(LEFT + FUN * yp, 8), 4 + y, base + yp)
    for yp in range(1, 4):
        send_terms(2 + yp, FUN * yp - 16, 8 + y, base - RING + yp)
    for yp in range(0, 3):
        send_terms(6 + yp, 176 + FUN * yp, y, base + RING + yp)

    for copy in v_copies:
        if copy is v_copies[2]:
            copy.wait()
        else:
            copy.wait_recv()
    for k in range(7):
        pot_rows[BOX * k : BOX * k + BOX, :] = v_win[k].astype(F32)[0:BOX]
    pot_rows[7 * BOX : 128, :] = jnp.zeros((128 - 7 * BOX, 1024), F32)

    near_rows = pot_rows[...].astype(BF)
    row_of = lax.broadcasted_iota(jnp.int32, (128, FRAME), 0)
    for j in range(3):
        select = (row_of == starts[pl.ds(LEFT // 8 + 3 * y + j, 1), :]).astype(F32).astype(BF)
        local = lax.dot_general(select, near_rows, (((0,), (0,)), ((), ())), preferred_element_type=F32)
        pot_own[8 * j : 8 * j + 8] = local.reshape(8, 4, 8, 1024)

    def wait_terms(slot):
        pltpu.make_async_copy(terms.at[slot], terms.at[slot], s_recv.at[slot]).wait()

    sums[0] = jnp.zeros((FUN, FRAME), F32)
    sums[2] = jnp.zeros((FUN, FRAME), F32)
    sums[1] = gram[my_rows, :]
    for k in range(1, 4):
        slot = 4 + lax.rem(y + k, RING)
        wait_terms(slot)
        sums[1] += terms[slot]

    @pl.when(y <= 2)
    def _():
        for ys in range(RING):
            wait_terms(ys)
        sums[0] = terms[0] + terms[1] + terms[2] + terms[3]

    @pl.when(y >= 1)
    def _():
        for ys in range(RING):
            wait_terms(8 + ys)
        sums[2] = terms[8] + terms[9] + terms[10] + terms[11]

    pad = jnp.zeros((FUN, FRAME), F32)
    wide = jnp.concatenate([sums[0], pad], axis=1)
    wide += pltpu.roll(jnp.concatenate([sums[1], pad], axis=1), 96, 1)
    wide += pltpu.roll(jnp.concatenate([sums[2], pad], axis=1), 192, 1)
    lane = lax.broadcasted_iota(jnp.int32, (FUN, 512), 1)
    sub = lax.broadcasted_iota(jnp.int32, (FUN, 512), 0)
    fixed = (1.5 * (lane == sub + (FUN * y + 176)).astype(F32) - 0.5 * wide)
    rows_out[0] = fixed[:, 0:256].astype(BF)
    rows_out[1] = pltpu.roll(fixed, 512 - 96, 1)[:, 0:256].astype(BF)
    rows_out[2] = pltpu.roll(fixed, 512 - 192, 1)[:, 0:256].astype(BF)

    c_copies = []

    def send_rows(n, which, slot, target):
        copy = pltpu.make_async_remote_copy(
            src_ref=rows_out.at[which],
            dst_ref=rows_in.at[slot],
            send_sem=c_send.at[n],
            recv_sem=c_recv.at[slot],
            device_id=dev(target),
            device_id_type=MESH,
        )
        copy.start()
        return copy

    own_rows = [
        send_rows(k - 1, 1, 4 + y, base + lax.rem(y + k, RING)) for k in range(1, 4)
    ]

    @pl.when(y <= 2)
    def _():
        for yp in range(RING):
            send_rows(3 + yp, 0, 8 + y, base - RING + yp)

    @pl.when(y >= 1)
    def _():
        for yp in range(RING):
            send_rows(7 + yp, 2, y, base + RING + yp)

    band = pltpu.roll(wide, 512 - 49 - FUN * y, 1)
    for bit in range(5):
        moved = pltpu.roll(band, 512 - (1 << bit), 1)
        band = jnp.where(jnp.bitwise_and(sub, 1 << bit) != 0, moved, band)
    gram_out[...] = jnp.where(lane[:, 0:256] == 255, 0.0, band[:, 0:256])

    def wait_rows(slot):
        pltpu.make_async_copy(rows_in.at[slot], rows_in.at[slot], c_recv.at[slot]).wait()

    mixing[0:16, :] = jnp.zeros((16, FRAME), F32)
    mixing[240:256, :] = jnp.zeros((16, FRAME), F32)
    mixing[my_rows, :] = rows_out[1].astype(F32)
    for k in range(1, 4):
        ys = lax.rem(y + k, RING)
        wait_rows(4 + ys)
        mixing[pl.ds(pl.multiple_of(LEFT + FUN * ys, 8), FUN), :] = rows_in[4 + ys].astype(F32)
    for ys in range(0, 3):
        wait_rows(8 + ys)
        mixing[176 + FUN * ys : 200 + FUN * ys, :] = rows_in[8 + ys].astype(F32)
    for ys in range(1, 4):
        wait_rows(ys)
        mixing[FUN * ys - 16 : FUN * ys + 8, :] = rows_in[ys].astype(F32)

    def mix_step(step, carry):
        for part in range(4):
            slot = 4 * step + part
            same_lo, same_hi = same_box(slot)
            mix = jnp.concatenate(
                [jnp.where(same_lo, mixing[:, 0:128], 0.0), jnp.where(same_hi, mixing[:, 128:256], 0.0)], axis=1
            ).astype(BF)
            slots[slot] = jnp.dot(mix, slots[slot], preferred_element_type=F32).astype(BF)
        return carry

    lax.fori_loop(0, SUP // 4, mix_step, 0)

    for copy in forwards:
        copy.wait_send()

    def out_of_slots(pair, carry):
        both = slots[:, pl.ds(pl.multiple_of(16 * pair, 16), 16), :].astype(F32)
        for half in range(2):
            octet = 2 * pair + half
            select = (row_id == meta[pl.ds(32 + octet, 1), :]).astype(F32).astype(BF)
            part = both[:, 8 * half : 8 * half + 8, :].reshape(FRAME, SLICE).astype(BF)
            out = jnp.dot(select, part, preferred_element_type=F32)
            frame[pl.ds(pl.multiple_of(8 * octet, 8), 8)] = out.reshape(8, 4, 8, SLICE).astype(BF)
        return carry

    lax.fori_loop(1, 5, out_of_slots, 0)
    lax.fori_loop(11, 15, out_of_slots, 0)
    backs = (back_a, back_b, back_c, back_d)
    x_backs = []
    for n, (src, q, nq, dst, to) in enumerate(FORWARD):
        copy = pltpu.make_async_remote_copy(
            src_ref=frame.at[pl.ds(dst, 32), pl.ds(q, nq)],
            dst_ref=backs[n],
            send_sem=bx_send.at[n],
            recv_sem=bx_recv.at[n],
            device_id=dev(me - RING * to),
            device_id_type=MESH,
        )
        copy.start()
        x_backs.append(copy)
    lax.fori_loop(5, 11, out_of_slots, 0)

    lanes = pl.ds(pl.multiple_of(y * SLICE, SLICE), SLICE)
    y_backs = []

    def quarters(octet):
        unit = lax.div(octet, 4)
        clean = 2 - unit
        first = 2 * lax.div(unit, 2)
        second = 3 - 2 * lax.div(3 - unit, 3)
        return ((clean, 2),), ((first, 1), (second, 1))

    def send_home(which):
        for k in (1, 3, 2, 0):
            yp = lax.rem(y + k, RING)
            for j in range(3):
                for n, (q, nq) in enumerate(quarters(3 * yp + j)[which]):
                    src = frame.at[pl.ds(pl.multiple_of(LEFT + FUN * yp + 8 * j, 8), 8), pl.ds(q, nq)]
                    dst = y_in.at[pl.ds(8 * j, 8), pl.ds(q, nq), :, lanes]
                    if k == 0:
                        pltpu.make_async_copy(src, dst, by_recv.at[y, j, which + n]).start()
                        continue
                    copy = pltpu.make_async_remote_copy(
                        src_ref=src,
                        dst_ref=dst,
                        send_sem=by_send.at[k - 1, j, which + n],
                        recv_sem=by_recv.at[y, j, which + n],
                        device_id=dev(base + yp),
                        device_id_type=MESH,
                    )
                    copy.start()
                    y_backs.append(copy)

    send_home(0)
    for n, (src, q, nq, dst, to) in enumerate(FORWARD):
        x_backs[n].wait_recv()
        mine = frame[src : src + 32, q : q + nq].astype(F32)
        frame[src : src + 32, q : q + nq] = (mine + backs[n][...].astype(F32)).astype(BF)
    send_home(1)

    kin_copy.wait()
    out_copies = []
    for which in range(2):
        for j in range(3):
            octs = quarters(3 * y + j)[which]
            for n, (q, nq) in enumerate(octs):
                for ys in range(RING):
                    part = y_in.at[pl.ds(8 * j, 8), pl.ds(q, nq), :, pl.ds(ys * SLICE, SLICE)]
                    pltpu.make_async_copy(part, part, by_recv.at[ys, j, which + n]).wait()
                rows = 8 * 8 * nq
                at = 128 * j + rows * n
                piece = y_in[8 * j : 8 * j + 8, pl.ds(q, nq)].astype(F32).reshape(rows, 1024)
                x_in[at : at + rows, :] = piece.astype(BF)
        for t in range(4):
            cols = slice(256 * t, 256 * t + 256)
            applied = jnp.dot(x_in[...], kin[:, cols], preferred_element_type=F32)
            for j in range(3):
                octs = quarters(3 * y + j)[which]
                for n, (q, nq) in enumerate(octs):
                    rows = 8 * 8 * nq
                    at = 128 * j + rows * n
                    local = pot_own[8 * j : 8 * j + 8, pl.ds(q, nq), :, cols].reshape(rows, 256)
                    res = applied[at : at + rows] + local * x_in[at : at + rows, cols].astype(F32)
                    y_res[8 * j : 8 * j + 8, pl.ds(q, nq), :, cols] = res.reshape(8, nq, 8, 256).astype(BF)
        for j in range(3):
            octs = quarters(3 * y + j)[which]
            for n, (q, nq) in enumerate(octs):
                copy = pltpu.make_async_copy(
                    y_res.at[pl.ds(8 * j, 8), pl.ds(q, nq)],
                    out.at[pl.ds(8 * j, 8), pl.ds(q, nq)],
                    out_sem.at[j, which + n],
                )
                copy.start()
                out_copies.append(copy)

    for copy in started:
        copy.wait_send()
    for k, copy in enumerate(v_copies):
        if k != 2:
            copy.wait_send()
    for copy in s_copies:
        copy.wait_send()
    for copy in own_rows:
        copy.wait_send()

    @pl.when(y <= 2)
    def _():
        for yp in range(RING):
            pltpu.make_async_copy(rows_out.at[0], rows_out.at[0], c_send.at[3 + yp]).wait()

    @pl.when(y >= 1)
    def _():
        for yp in range(RING):
            pltpu.make_async_copy(rows_out.at[2], rows_out.at[2], c_send.at[7 + yp]).wait()

    for copy in x_backs:
        copy.wait_send()
    for copy in y_backs:
        copy.wait_send()
    for copy in out_copies:
        copy.wait()


def on_device(coeffs, centers, kinetic, potential):
    hbm = pl.BlockSpec(memory_space=pl.ANY)
    vmem = pl.BlockSpec(memory_space=pltpu.VMEM)
    dma = pltpu.SemaphoreType.DMA
    filtered, gram_band = pl.pallas_call(
        exchange_kernel,
        out_shape=(
            jax.ShapeDtypeStruct((FUN, 4, 8, 1024), BF),
            jax.ShapeDtypeStruct((FUN, FRAME), F32),
        ),
        in_specs=[hbm, hbm, vmem, vmem],
        out_specs=(hbm, vmem),
        scratch_shapes=[
            pltpu.VMEM((FRAME, 4, 8, SLICE), BF),
            pltpu.VMEM((SUP, FRAME, SLICE), BF),
            pltpu.VMEM((32, 2, 8, SLICE), BF),
            pltpu.VMEM((32, 2, 8, SLICE), BF),
            pltpu.VMEM((32, 1, 8, SLICE), BF),
            pltpu.VMEM((32, 1, 8, SLICE), BF),
            pltpu.VMEM((FRAME, FRAME), F32),
            pltpu.VMEM((12, FUN, FRAME), F32),
            pltpu.VMEM((3, FUN, FRAME), F32),
            pltpu.VMEM((3, FUN, FRAME), BF),
            pltpu.VMEM((12, FUN, FRAME), BF),
            pltpu.VMEM((FRAME, FRAME), F32),
            pltpu.VMEM((16, 1024), BF),
            pltpu.VMEM((FRAME, 128), jnp.int32),
            pltpu.VMEM((64, FRAME), jnp.int32),
            pltpu.VMEM((32, FRAME), jnp.int32),
            pltpu.VMEM((1024, 1024), BF),
            pltpu.VMEM((7, 16, 1024), BF),
            pltpu.VMEM((128, 1024), F32),
            pltpu.VMEM((FUN, 4, 8, 1024), F32),
            pltpu.VMEM((FUN, 4, 8, 1024), BF),
            pltpu.VMEM((384, 1024), BF),
            pltpu.VMEM((FUN, 4, 8, 1024), BF),
            dma((3, 4)), dma((4, 4)), dma((4,)), dma((4,)), dma((7,)), dma((7,)),
            dma((9,)), dma((12,)), dma((11,)), dma((12,)), dma((4,)), dma((4,)),
            dma((3, 3, 3)), dma((4, 3, 3)), dma, dma((3, 3)),
        ],
        compiler_params=pltpu.CompilerParams(collective_id=0, has_side_effects=True),
        name="exchange",
    )(coeffs.reshape(FUN, 4, 8, 1024), kinetic, potential, centers.reshape(FUN, 128))
    return filtered.reshape(FUN, SUP, 1024), gram_band


def solution(mesh):
    placed = (P(("func", "box"), None, None), P(), P(), P(("func", "box"), None))
    return jax.shard_map(
        on_device,
        mesh=mesh,
        in_specs=placed,
        out_specs=(P(("func", "box"), None, None), P(("func", "box"), None)),
        check_vma=False,
    )
```

```python
import jax
import jax.numpy as jnp
from jax import lax
from jax.experimental import pallas as pl
from jax.experimental.pallas import tpu as pltpu
from jax.sharding import PartitionSpec as P

MESH = pl.DeviceIdType.MESH
BF = jnp.bfloat16
F32 = jnp.float32

SUP = 32
FUN = 24
BOX = 12
RING = 4
OWN = FUN * RING
FRAME = 256
LEFT = 80
SLICE = 256
BOX_ALL = 1536
FUN_ALL = 3072
W_HALO = 4
W_OWN = 6
VOLUME = 1.0 / (32 * 1024)

HALO = (
    (80, 0, 2, 176, -1),
    (144, 2, 2, 48, 1),
    (112, 0, 1, 208, -1),
    (112, 3, 1, 16, 1),
)
FORWARD = (
    (0, 0, 0, 24, -1),
    (3, 3, 0, 24, 1),
    (1, 0, 0, 24, -1),
    (2, 3, 0, 24, 1),
    (0, 1, 0, 24, -1),
    (3, 2, 0, 24, 1),
    (2, 0, 0, 16, -1),
    (1, 3, 8, 16, 1),
    (1, 1, 0, 8, -1),
    (2, 2, 16, 8, 1),
)


def exchange_kernel(
    coeffs, kinetic, pot, lanes_in, out, gram_out,
    frame, slots, gram_out_rows, back_a, back_b, back_c, back_d, gram, terms, sums, rows_out, rows_in, mixing, potb, boxes,
    meta, starts, kin, v_win, pot_rows, pot_own, y_in, x_in, y_res,
    y_send, y_recv, x_send, x_recv, v_send, v_recv, s_send, s_recv, c_send, c_recv, bx_send, bx_recv,
    by_send, by_recv, kin_sem, out_sem,
):
    me = lax.axis_index("func") * 16 + lax.axis_index("box")
    y = lax.rem(me, RING)
    base = me - y

    def dev(linear):
        wrapped = lax.rem(linear + 128, 128)
        return (lax.div(wrapped, 16), lax.rem(wrapped, 16))

    barrier = pltpu.get_barrier_semaphore()
    partners = [base + lax.rem(y + k, RING) for k in range(1, RING)] + [me + RING, me - RING]
    for partner in partners:
        pl.semaphore_signal(barrier, inc=1, device_id=dev(partner), device_id_type=MESH)

    kin_copy = pltpu.make_async_copy(kinetic, kin, kin_sem)
    kin_copy.start()

    frame[16:48, 0:3] = jnp.zeros((32, 3, 8, SLICE), BF)
    frame[48:80, 0:2] = jnp.zeros((32, 2, 8, SLICE), BF)
    frame[176:208, 2:4] = jnp.zeros((32, 2, 8, SLICE), BF)
    frame[208:240, 1:4] = jnp.zeros((32, 3, 8, SLICE), BF)
    slots[:, 0:16, :] = jnp.zeros((SUP, 16, SLICE), BF)
    slots[:, 240:256, :] = jnp.zeros((SUP, 16, SLICE), BF)
    potb[0:BOX, :] = pot[...].astype(BF)
    potb[BOX:16, :] = jnp.zeros((16 - BOX, 1024), BF)
    pl.semaphore_wait(barrier, len(partners))

    started = []

    my_rows = pl.ds(pl.multiple_of(LEFT + FUN * y, 8), FUN)
    high = lax.div(y, 2)
    inner = lax.rem(lax.div(y + 1, 2), 2)

    for p in range(4):
        q0 = p + inner * ((0, 3, 1, 2)[p] - p)
        q = q0 + high * (3 - 2 * q0)
        for k in (1, 3, 2):
            yp = lax.rem(y + k, RING)
            copy = pltpu.make_async_remote_copy(
                src_ref=coeffs.at[:, q, :, pl.ds(pl.multiple_of(yp * SLICE, SLICE), SLICE)],
                dst_ref=frame.at[my_rows, q],
                send_sem=y_send.at[k - 1, p],
                recv_sem=y_recv.at[y, q],
                device_id=dev(base + yp),
                device_id_type=MESH,
            )
            copy.start()
            started.append(copy)
        pltpu.make_async_copy(
            coeffs.at[:, q, :, pl.ds(pl.multiple_of(y * SLICE, SLICE), SLICE)],
            frame.at[my_rows, q],
            y_recv.at[y, q],
        ).start()

    ring = lax.div(me, RING)
    flat = ring * OWN - LEFT + FUN_ALL
    top_line = lax.div(flat, 128)
    lines = [lanes_in[pl.ds(lax.rem(top_line + k, FUN_ALL // 128), 1), :] for k in range(3)]
    near = pltpu.roll(jnp.concatenate(lines, axis=1), 384 - lax.rem(flat, 128), 1)[:, 0:FRAME]
    row_lane = lax.broadcasted_iota(jnp.int32, (1, FRAME), 1)

    def pick(row, lane_at):
        return jnp.sum(jnp.where(row_lane == lane_at, row, 0), axis=1, keepdims=True)

    rel_row = near - pick(near, LEFT) + OWN
    rel_row = jnp.where(rel_row < 0, rel_row + BOX_ALL, rel_row)
    rel_row = jnp.where(rel_row >= BOX_ALL, rel_row - BOX_ALL, rel_row)
    low_row = OWN + 16
    top_row = pick(rel_row, LEFT + OWN - 1) + 16
    row_id = lax.broadcasted_iota(jnp.int32, (FRAME, FRAME), 0)
    col_id = lax.broadcasted_iota(jnp.int32, (FRAME, FRAME), 1)
    rel_tile = jnp.broadcast_to(rel_row, (FRAME, FRAME))
    rel_col = jnp.sum(
        jnp.where(row_id == col_id, rel_tile.astype(F32), 0.0), axis=1, keepdims=True
    ).astype(jnp.int32)
    boxes[...] = jnp.broadcast_to(rel_col, (FRAME, 128))
    sub_o = lax.broadcasted_iota(jnp.int32, (32, FRAME), 0)
    lane_o = lax.broadcasted_iota(jnp.int32, (32, FRAME), 1)
    rest_row = jnp.bitwise_and(rel_row, SUP - 1)
    spread = jnp.where(
        lax.shift_right_logical(lane_o, 3) == sub_o, jnp.broadcast_to(rest_row, (32, FRAME)), 0
    ).astype(F32).astype(BF)
    in_octet = jnp.bitwise_and(row_id, 7)
    by_fun = (in_octet == lax.shift_right_logical(col_id, 5)).astype(F32).astype(BF)
    by_low = (in_octet == jnp.bitwise_and(col_id, 7)).astype(F32).astype(BF)
    rest_fun = jnp.dot(spread, by_fun, preferred_element_type=F32).astype(jnp.int32)
    rest_low = jnp.dot(spread, by_low, preferred_element_type=F32).astype(jnp.int32)
    meta[0:32, :] = jnp.bitwise_and(rest_fun + lane_o, SUP - 1) * 8 + lax.shift_right_logical(lane_o, 5)
    meta[32:64, :] = jnp.bitwise_and(lane_o, 7) * SUP + jnp.bitwise_and(
        lax.shift_right_logical(lane_o, 3) - rest_low, SUP - 1
    )

    start_row = near - BOX * (me - 2)
    start_row = jnp.where(start_row < 0, start_row + BOX_ALL, start_row)
    start_row = jnp.where(start_row >= BOX_ALL, start_row - BOX_ALL, start_row)
    start_row = jnp.minimum(start_row, 127)
    spread = jnp.where(
        lax.shift_right_logical(lane_o, 3) == sub_o, jnp.broadcast_to(start_row, (32, FRAME)), 0
    ).astype(F32).astype(BF)
    starts[...] = jnp.dot(spread, by_fun, preferred_element_type=F32).astype(jnp.int32) + jnp.bitwise_and(
        lane_o, SUP - 1
    )

    arrived = set()

    def wait_piece(ys, q):
        if (ys, q) in arrived:
            return
        arrived.add((ys, q))
        piece = frame.at[pl.ds(LEFT + FUN * ys, FUN), q]
        pltpu.make_async_copy(piece, piece, y_recv.at[ys, q]).wait()

    forwards = []
    for n, (ys, q, first, count, to) in enumerate(FORWARD):
        wait_piece(ys, q)
        src = LEFT + FUN * ys + first
        copy = pltpu.make_async_remote_copy(
            src_ref=frame.at[pl.ds(src, count), q],
            dst_ref=frame.at[pl.ds(src - OWN * to, count), q],
            send_sem=x_send.at[n],
            recv_sem=x_recv.at[n],
            device_id=dev(me + RING * to),
            device_id_type=MESH,
        )
        copy.start()
        forwards.append(copy)

    def pairs(step_of, first, count, width):
        def several(step, carry):
            for k in range(width):
                step_of(first + width * step + k, carry)
            return carry

        lax.fori_loop(0, count // width, several, 0)

    def into_slots(pair, carry):
        parts = []
        for half in range(2):
            octet = 2 * pair + half
            select = (row_id == meta[pl.ds(octet, 1), :]).astype(F32).astype(BF)
            raw = frame[pl.ds(pl.multiple_of(8 * octet, 8), 8)]
            raw = raw.astype(F32).reshape(FRAME, SLICE).astype(BF)
            out = jnp.dot(select, raw, preferred_element_type=F32)
            parts.append(out.reshape(SUP, 8, SLICE))
        both = jnp.concatenate(parts, axis=1).astype(BF)
        slots[:, pl.ds(pl.multiple_of(16 * pair, 16), 16), :] = both
        return carry

    for copy in forwards:
        copy.wait_recv()
    pairs(into_slots, 1, 4, W_HALO)
    pairs(into_slots, 11, 4, W_HALO)
    for ys in range(RING):
        for q in range(4):
            wait_piece(ys, q)

    v_copies = []
    for o in range(-2, 5):
        if o == 0:
            copy = pltpu.make_async_copy(potb, v_win.at[2], v_recv.at[2])
        else:
            copy = pltpu.make_async_remote_copy(
                src_ref=potb,
                dst_ref=v_win.at[o + 2],
                send_sem=v_send.at[o + 2],
                recv_sem=v_recv.at[o + 2],
                device_id=dev(me - o),
                device_id_type=MESH,
            )
        copy.start()
        v_copies.append(copy)

    pairs(into_slots, 5, 6, W_OWN)

    def same_box(slot):
        box_row = rel_row + jnp.bitwise_and(slot - rel_row, SUP - 1)
        owned = jnp.logical_and(box_row >= low_row, box_row <= top_row)
        box_row = jnp.where(owned, box_row, -1)
        col = boxes[...]
        box_col = col + jnp.bitwise_and(slot - col, SUP - 1)
        return box_col == box_row[:, 0:128], box_col == box_row[:, 128:256]

    gram[...] = jnp.zeros((FRAME, FRAME), F32)

    def gram_step(step, carry):
        lo, hi = gram[:, 0:128], gram[:, 128:256]
        for part in range(4):
            slot = 4 * step + part
            held = slots[slot]
            prod = lax.dot_general(held, held, (((1,), (1,)), ((), ())), preferred_element_type=F32)
            same_lo, same_hi = same_box(slot)
            lo = lo + jnp.where(same_lo, prod[:, 0:128], 0.0)
            hi = hi + jnp.where(same_hi, prod[:, 128:256], 0.0)
        gram[:, 0:128] = lo
        gram[:, 128:256] = hi
        return carry

    lax.fori_loop(0, SUP // 4, gram_step, 0)
    scaled = gram[...] * VOLUME
    gram[...] = scaled
    gram_out_rows[...] = scaled.reshape(FRAME // 8, 8, FRAME).astype(BF)

    s_copies = []

    def send_terms(n, start, slot, target):
        copy = pltpu.make_async_remote_copy(
            src_ref=gram_out_rows.at[pl.ds(start, FUN // 8)],
            dst_ref=terms.at[slot],
            send_sem=s_send.at[n],
            recv_sem=s_recv.at[slot],
            device_id=dev(target),
            device_id_type=MESH,
        )
        copy.start()
        s_copies.append(copy)

    for yp in range(1, 4):
        send_terms(2 + yp, 3 * yp - 2, 8 + y, base - RING + yp)
    for yp in range(0, 3):
        send_terms(6 + yp, 22 + 3 * yp, y, base + RING + yp)
    for k in range(1, 4):
        yp = lax.rem(y + k, RING)
        send_terms(k - 1, LEFT // 8 + 3 * yp, 4 + y, base + yp)

    for copy in v_copies:
        if copy is v_copies[2]:
            copy.wait()
        else:
            copy.wait_recv()
    for k in range(7):
        pot_rows[BOX * k : BOX * k + BOX, :] = v_win[k].astype(F32)[0:BOX]
    pot_rows[7 * BOX : 128, :] = jnp.zeros((128 - 7 * BOX, 1024), F32)

    near_rows = pot_rows[...].astype(BF)
    row_of = lax.broadcasted_iota(jnp.int32, (128, FRAME), 0)
    for j in range(3):
        select = (row_of == starts[pl.ds(LEFT // 8 + 3 * y + j, 1), :]).astype(F32).astype(BF)
        local = lax.dot_general(select, near_rows, (((0,), (0,)), ((), ())), preferred_element_type=F32)
        pot_own[8 * j : 8 * j + 8] = local.reshape(8, 4, 8, 1024)

    def wait_terms(slot):
        pltpu.make_async_copy(terms.at[slot], terms.at[slot], s_recv.at[slot]).wait()

    def arrived_terms(slot):
        return terms[slot].astype(F32).reshape(FUN, FRAME)

    sums[0] = jnp.zeros((FUN, FRAME), F32)
    sums[2] = jnp.zeros((FUN, FRAME), F32)
    sums[1] = gram[my_rows, :]
    for k in range(1, 4):
        slot = 4 + lax.rem(y + k, RING)
        wait_terms(slot)
        sums[1] += arrived_terms(slot)

    @pl.when(y <= 2)
    def _():
        for ys in range(RING):
            wait_terms(ys)
        sums[0] = arrived_terms(0) + arrived_terms(1) + arrived_terms(2) + arrived_terms(3)

    @pl.when(y >= 1)
    def _():
        for ys in range(RING):
            wait_terms(8 + ys)
        sums[2] = arrived_terms(8) + arrived_terms(9) + arrived_terms(10) + arrived_terms(11)

    pad = jnp.zeros((FUN, FRAME), F32)
    wide = jnp.concatenate([sums[0], pad], axis=1)
    wide += pltpu.roll(jnp.concatenate([sums[1], pad], axis=1), 96, 1)
    wide += pltpu.roll(jnp.concatenate([sums[2], pad], axis=1), 192, 1)
    lane = lax.broadcasted_iota(jnp.int32, (FUN, 512), 1)
    sub = lax.broadcasted_iota(jnp.int32, (FUN, 512), 0)
    fixed = (1.5 * (lane == sub + (FUN * y + 176)).astype(F32) - 0.5 * wide)
    rows_out[0] = fixed[:, 0:256].astype(BF)
    rows_out[1] = pltpu.roll(fixed, 512 - 96, 1)[:, 0:256].astype(BF)
    rows_out[2] = pltpu.roll(fixed, 512 - 192, 1)[:, 0:256].astype(BF)

    c_copies = []

    def send_rows(n, which, slot, target):
        copy = pltpu.make_async_remote_copy(
            src_ref=rows_out.at[which],
            dst_ref=rows_in.at[slot],
            send_sem=c_send.at[n],
            recv_sem=c_recv.at[slot],
            device_id=dev(target),
            device_id_type=MESH,
        )
        copy.start()
        return copy

    own_rows = [
        send_rows(k - 1, 1, 4 + y, base + lax.rem(y + k, RING)) for k in range(1, 4)
    ]

    @pl.when(y <= 2)
    def _():
        for yp in range(RING):
            send_rows(3 + yp, 0, 8 + y, base - RING + yp)

    @pl.when(y >= 1)
    def _():
        for yp in range(RING):
            send_rows(7 + yp, 2, y, base + RING + yp)

    band = pltpu.roll(wide, 512 - 49 - FUN * y, 1)
    for bit in range(5):
        moved = pltpu.roll(band, 512 - (1 << bit), 1)
        band = jnp.where(jnp.bitwise_and(sub, 1 << bit) != 0, moved, band)
    gram_out[...] = jnp.where(lane[:, 0:256] == 255, 0.0, band[:, 0:256])

    def wait_rows(slot):
        pltpu.make_async_copy(rows_in.at[slot], rows_in.at[slot], c_recv.at[slot]).wait()

    mixing[0:16, :] = jnp.zeros((16, FRAME), F32)
    mixing[240:256, :] = jnp.zeros((16, FRAME), F32)
    mixing[my_rows, :] = rows_out[1].astype(F32)
    for k in range(1, 4):
        ys = lax.rem(y + k, RING)
        wait_rows(4 + ys)
        mixing[pl.ds(pl.multiple_of(LEFT + FUN * ys, 8), FUN), :] = rows_in[4 + ys].astype(F32)
    for ys in range(0, 3):
        wait_rows(8 + ys)
        mixing[176 + FUN * ys : 200 + FUN * ys, :] = rows_in[8 + ys].astype(F32)
    for ys in range(1, 4):
        wait_rows(ys)
        mixing[FUN * ys - 16 : FUN * ys + 8, :] = rows_in[ys].astype(F32)

    def mix_step(step, carry):
        for part in range(4):
            slot = 4 * step + part
            same_lo, same_hi = same_box(slot)
            mix = jnp.concatenate(
                [jnp.where(same_lo, mixing[:, 0:128], 0.0), jnp.where(same_hi, mixing[:, 128:256], 0.0)], axis=1
            ).astype(BF)
            slots[slot] = jnp.dot(mix, slots[slot], preferred_element_type=F32).astype(BF)
        return carry

    lax.fori_loop(0, SUP // 4, mix_step, 0)

    for copy in forwards:
        copy.wait_send()

    def out_of_slots(pair, carry):
        both = slots[:, pl.ds(pl.multiple_of(16 * pair, 16), 16), :].astype(F32)
        for half in range(2):
            octet = 2 * pair + half
            select = (row_id == meta[pl.ds(32 + octet, 1), :]).astype(F32).astype(BF)
            part = both[:, 8 * half : 8 * half + 8, :].reshape(FRAME, SLICE).astype(BF)
            out = jnp.dot(select, part, preferred_element_type=F32)
            frame[pl.ds(pl.multiple_of(8 * octet, 8), 8)] = out.reshape(8, 4, 8, SLICE).astype(BF)
        return carry

    pairs(out_of_slots, 1, 4, W_HALO)
    pairs(out_of_slots, 11, 4, W_HALO)
    backs = (back_a, back_b, back_c, back_d)
    x_backs = []
    for n, (src, q, nq, dst, to) in enumerate(HALO):
        copy = pltpu.make_async_remote_copy(
            src_ref=frame.at[pl.ds(dst, 32), pl.ds(q, nq)],
            dst_ref=backs[n],
            send_sem=bx_send.at[n],
            recv_sem=bx_recv.at[n],
            device_id=dev(me - RING * to),
            device_id_type=MESH,
        )
        copy.start()
        x_backs.append(copy)
    pairs(out_of_slots, 5, 6, W_OWN)

    lanes = pl.ds(pl.multiple_of(y * SLICE, SLICE), SLICE)
    y_backs = []

    def quarters(octet):
        unit = lax.div(octet, 4)
        clean = 2 - unit
        first = 2 * lax.div(unit, 2)
        second = 3 - 2 * lax.div(3 - unit, 3)
        return ((clean, 2),), ((first, 1), (second, 1))

    def send_home(which):
        for k in (1, 3, 2, 0):
            yp = lax.rem(y + k, RING)
            for j in range(3):
                for n, (q, nq) in enumerate(quarters(3 * yp + j)[which]):
                    src = frame.at[pl.ds(pl.multiple_of(LEFT + FUN * yp + 8 * j, 8), 8), pl.ds(q, nq)]
                    dst = y_in.at[pl.ds(8 * j, 8), pl.ds(q, nq), :, lanes]
                    if k == 0:
                        pltpu.make_async_copy(src, dst, by_recv.at[y, j, which + n]).start()
                        continue
                    copy = pltpu.make_async_remote_copy(
                        src_ref=src,
                        dst_ref=dst,
                        send_sem=by_send.at[k - 1, j, which + n],
                        recv_sem=by_recv.at[y, j, which + n],
                        device_id=dev(base + yp),
                        device_id_type=MESH,
                    )
                    copy.start()
                    y_backs.append(copy)

    send_home(0)
    for n, (src, q, nq, dst, to) in enumerate(HALO):
        x_backs[n].wait_recv()
        mine = frame[src : src + 32, q : q + nq].astype(F32)
        frame[src : src + 32, q : q + nq] = (mine + backs[n][...].astype(F32)).astype(BF)
    send_home(1)

    kin_copy.wait()
    out_copies = []
    for which in range(2):
        for j in range(3):
            octs = quarters(3 * y + j)[which]
            for n, (q, nq) in enumerate(octs):
                for ys in range(RING):
                    part = y_in.at[pl.ds(8 * j, 8), pl.ds(q, nq), :, pl.ds(ys * SLICE, SLICE)]
                    pltpu.make_async_copy(part, part, by_recv.at[ys, j, which + n]).wait()
                rows = 8 * 8 * nq
                at = 128 * j + rows * n
                piece = y_in[8 * j : 8 * j + 8, pl.ds(q, nq)].astype(F32).reshape(rows, 1024)
                x_in[at : at + rows, :] = piece.astype(BF)
        for t in range(4):
            cols = slice(256 * t, 256 * t + 256)
            applied = jnp.dot(x_in[...], kin[:, cols], preferred_element_type=F32)
            for j in range(3):
                octs = quarters(3 * y + j)[which]
                for n, (q, nq) in enumerate(octs):
                    rows = 8 * 8 * nq
                    at = 128 * j + rows * n
                    local = pot_own[8 * j : 8 * j + 8, pl.ds(q, nq), :, cols].reshape(rows, 256)
                    res = applied[at : at + rows] + local * x_in[at : at + rows, cols].astype(F32)
                    y_res[8 * j : 8 * j + 8, pl.ds(q, nq), :, cols] = res.reshape(8, nq, 8, 256).astype(BF)
        for j in range(3):
            octs = quarters(3 * y + j)[which]
            for n, (q, nq) in enumerate(octs):
                copy = pltpu.make_async_copy(
                    y_res.at[pl.ds(8 * j, 8), pl.ds(q, nq)],
                    out.at[pl.ds(8 * j, 8), pl.ds(q, nq)],
                    out_sem.at[j, which + n],
                )
                copy.start()
                out_copies.append(copy)

    for copy in started:
        copy.wait_send()
    for k, copy in enumerate(v_copies):
        if k != 2:
            copy.wait_send()
    for copy in s_copies:
        copy.wait_send()
    for copy in own_rows:
        copy.wait_send()

    @pl.when(y <= 2)
    def _():
        for yp in range(RING):
            pltpu.make_async_copy(rows_out.at[0], rows_out.at[0], c_send.at[3 + yp]).wait()

    @pl.when(y >= 1)
    def _():
        for yp in range(RING):
            pltpu.make_async_copy(rows_out.at[2], rows_out.at[2], c_send.at[7 + yp]).wait()

    for copy in x_backs:
        copy.wait_send()
    for copy in y_backs:
        copy.wait_send()
    for copy in out_copies:
        copy.wait()


def on_device(coeffs, centers, kinetic, potential):
    hbm = pl.BlockSpec(memory_space=pl.ANY)
    vmem = pl.BlockSpec(memory_space=pltpu.VMEM)
    dma = pltpu.SemaphoreType.DMA
    filtered, gram_band = pl.pallas_call(
        exchange_kernel,
        out_shape=(
            jax.ShapeDtypeStruct((FUN, 4, 8, 1024), BF),
            jax.ShapeDtypeStruct((FUN, FRAME), F32),
        ),
        in_specs=[hbm, hbm, vmem, vmem],
        out_specs=(hbm, vmem),
        scratch_shapes=[
            pltpu.VMEM((FRAME, 4, 8, SLICE), BF),
            pltpu.VMEM((SUP, FRAME, SLICE), BF),
            pltpu.VMEM((FRAME // 8, 8, FRAME), BF),
            pltpu.VMEM((32, 2, 8, SLICE), BF),
            pltpu.VMEM((32, 2, 8, SLICE), BF),
            pltpu.VMEM((32, 1, 8, SLICE), BF),
            pltpu.VMEM((32, 1, 8, SLICE), BF),
            pltpu.VMEM((FRAME, FRAME), F32),
            pltpu.VMEM((12, FUN // 8, 8, FRAME), BF),
            pltpu.VMEM((3, FUN, FRAME), F32),
            pltpu.VMEM((3, FUN, FRAME), BF),
            pltpu.VMEM((12, FUN, FRAME), BF),
            pltpu.VMEM((FRAME, FRAME), F32),
            pltpu.VMEM((16, 1024), BF),
            pltpu.VMEM((FRAME, 128), jnp.int32),
            pltpu.VMEM((64, FRAME), jnp.int32),
            pltpu.VMEM((32, FRAME), jnp.int32),
            pltpu.VMEM((1024, 1024), BF),
            pltpu.VMEM((7, 16, 1024), BF),
            pltpu.VMEM((128, 1024), F32),
            pltpu.VMEM((FUN, 4, 8, 1024), F32),
            pltpu.VMEM((FUN, 4, 8, 1024), BF),
            pltpu.VMEM((384, 1024), BF),
            pltpu.VMEM((FUN, 4, 8, 1024), BF),
            dma((3, 4)), dma((4, 4)), dma((10,)), dma((10,)), dma((7,)), dma((7,)),
            dma((9,)), dma((12,)), dma((11,)), dma((12,)), dma((4,)), dma((4,)),
            dma((3, 3, 3)), dma((4, 3, 3)), dma, dma((3, 3)),
        ],
        compiler_params=pltpu.CompilerParams(collective_id=0, has_side_effects=True),
        name="exchange",
    )(coeffs.reshape(FUN, 4, 8, 1024), kinetic, potential, centers.reshape(FUN, 128))
    return filtered.reshape(FUN, SUP, 1024), gram_band


def solution(mesh):
    placed = (P(("func", "box"), None, None), P(), P(), P(("func", "box"), None))
    return jax.shard_map(
        on_device,
        mesh=mesh,
        in_specs=placed,
        out_specs=(P(("func", "box"), None, None), P(("func", "box"), None)),
        check_vma=False,
    )
```

```python
import jax
import jax.numpy as jnp
from jax import lax
from jax.experimental import pallas as pl
from jax.experimental.pallas import tpu as pltpu
from jax.sharding import PartitionSpec as P

MESH = pl.DeviceIdType.MESH
BF = jnp.bfloat16
F32 = jnp.float32

SUP = 32
FUN = 24
BOX = 12
RING = 4
OWN = FUN * RING
FRAME = 256
LEFT = 80
SLICE = 256
BOX_ALL = 1536
FUN_ALL = 3072
W_HALO = 4
W_OWN = 6
VOLUME = 1.0 / (32 * 1024)

HALO = (
    (80, 0, 2, 176, -1),
    (144, 2, 2, 48, 1),
    (112, 0, 1, 208, -1),
    (112, 3, 1, 16, 1),
)
FORWARD = (
    (0, 0, 0, 24, -1),
    (3, 3, 0, 24, 1),
    (1, 0, 0, 24, -1),
    (2, 3, 0, 24, 1),
    (0, 1, 0, 24, -1),
    (3, 2, 0, 24, 1),
    (2, 0, 0, 16, -1),
    (1, 3, 8, 16, 1),
    (1, 1, 0, 8, -1),
    (2, 2, 16, 8, 1),
)


def exchange_kernel(
    coeffs, kinetic, pot_hbm, lanes_hbm, out, gram_hbm,
    frame, slots, gram_out_rows, back_a, back_b, back_c, back_d, gram, terms, sums, rows_out, rows_in, mixing, potb, boxes,
    pot, lanes_in, gram_out, meta, starts, kin, v_win, pot_rows, pot_own, y_in, x_in, y_res,
    y_send, y_recv, x_send, x_recv, v_send, v_recv, s_send, s_recv, c_send, c_recv, bx_send, bx_recv,
    by_send, by_recv, kin_sem, out_sem,
):
    me = lax.axis_index("func") * 16 + lax.axis_index("box")
    y = lax.rem(me, RING)
    base = me - y

    def dev(linear):
        wrapped = lax.rem(linear + 128, 128)
        return (lax.div(wrapped, 16), lax.rem(wrapped, 16))

    barrier = pltpu.get_barrier_semaphore()
    partners = [base + lax.rem(y + k, RING) for k in range(1, RING)] + [me + RING, me - RING]
    for partner in partners:
        pl.semaphore_signal(barrier, inc=1, device_id=dev(partner), device_id_type=MESH)

    loads = [
        pltpu.make_async_copy(src, dst, kin_sem.at[n])
        for n, (src, dst) in enumerate(((lanes_hbm, lanes_in), (pot_hbm, pot), (kinetic, kin)))
    ]
    for copy in loads:
        copy.start()

    pl.semaphore_wait(barrier, len(partners))

    started = []

    my_rows = pl.ds(pl.multiple_of(LEFT + FUN * y, 8), FUN)
    high = lax.div(y, 2)
    inner = lax.rem(lax.div(y + 1, 2), 2)

    for p in range(4):
        q0 = p + inner * ((0, 3, 1, 2)[p] - p)
        q = q0 + high * (3 - 2 * q0)
        for k in (1, 3, 2):
            yp = lax.rem(y + k, RING)
            copy = pltpu.make_async_remote_copy(
                src_ref=coeffs.at[:, q, :, pl.ds(pl.multiple_of(yp * SLICE, SLICE), SLICE)],
                dst_ref=frame.at[my_rows, q],
                send_sem=y_send.at[k - 1, p],
                recv_sem=y_recv.at[y, q],
                device_id=dev(base + yp),
                device_id_type=MESH,
            )
            copy.start()
            started.append(copy)
        pltpu.make_async_copy(
            coeffs.at[:, q, :, pl.ds(pl.multiple_of(y * SLICE, SLICE), SLICE)],
            frame.at[my_rows, q],
            y_recv.at[y, q],
        ).start()

    frame[16:48, 0:3] = jnp.zeros((32, 3, 8, SLICE), BF)
    frame[48:80, 0:2] = jnp.zeros((32, 2, 8, SLICE), BF)
    frame[176:208, 2:4] = jnp.zeros((32, 2, 8, SLICE), BF)
    frame[208:240, 1:4] = jnp.zeros((32, 3, 8, SLICE), BF)
    slots[:, 0:16, :] = jnp.zeros((SUP, 16, SLICE), BF)
    slots[:, 240:256, :] = jnp.zeros((SUP, 16, SLICE), BF)

    loads[0].wait()
    ring = lax.div(me, RING)
    flat = ring * OWN - LEFT + FUN_ALL
    top_line = lax.div(flat, 128)
    lines = [lanes_in[pl.ds(lax.rem(top_line + k, FUN_ALL // 128), 1), :] for k in range(3)]
    near = pltpu.roll(jnp.concatenate(lines, axis=1), 384 - lax.rem(flat, 128), 1)[:, 0:FRAME]
    row_lane = lax.broadcasted_iota(jnp.int32, (1, FRAME), 1)

    def pick(row, lane_at):
        return jnp.sum(jnp.where(row_lane == lane_at, row, 0), axis=1, keepdims=True)

    rel_row = near - pick(near, LEFT) + OWN
    rel_row = jnp.where(rel_row < 0, rel_row + BOX_ALL, rel_row)
    rel_row = jnp.where(rel_row >= BOX_ALL, rel_row - BOX_ALL, rel_row)
    low_row = OWN + 16
    top_row = pick(rel_row, LEFT + OWN - 1) + 16
    row_id = lax.broadcasted_iota(jnp.int32, (FRAME, FRAME), 0)
    col_id = lax.broadcasted_iota(jnp.int32, (FRAME, FRAME), 1)
    rel_tile = jnp.broadcast_to(rel_row, (FRAME, FRAME))
    rel_col = jnp.sum(
        jnp.where(row_id == col_id, rel_tile.astype(F32), 0.0), axis=1, keepdims=True
    ).astype(jnp.int32)
    boxes[...] = jnp.broadcast_to(rel_col, (FRAME, 128))
    sub_o = lax.broadcasted_iota(jnp.int32, (32, FRAME), 0)
    lane_o = lax.broadcasted_iota(jnp.int32, (32, FRAME), 1)
    rest_row = jnp.bitwise_and(rel_row, SUP - 1)
    spread = jnp.where(
        lax.shift_right_logical(lane_o, 3) == sub_o, jnp.broadcast_to(rest_row, (32, FRAME)), 0
    ).astype(F32).astype(BF)
    in_octet = jnp.bitwise_and(row_id, 7)
    by_fun = (in_octet == lax.shift_right_logical(col_id, 5)).astype(F32).astype(BF)
    by_low = (in_octet == jnp.bitwise_and(col_id, 7)).astype(F32).astype(BF)
    rest_fun = jnp.dot(spread, by_fun, preferred_element_type=F32).astype(jnp.int32)
    rest_low = jnp.dot(spread, by_low, preferred_element_type=F32).astype(jnp.int32)
    meta[0:32, :] = jnp.bitwise_and(rest_fun + lane_o, SUP - 1) * 8 + lax.shift_right_logical(lane_o, 5)
    meta[32:64, :] = jnp.bitwise_and(lane_o, 7) * SUP + jnp.bitwise_and(
        lax.shift_right_logical(lane_o, 3) - rest_low, SUP - 1
    )

    start_row = near - BOX * (me - 2)
    start_row = jnp.where(start_row < 0, start_row + BOX_ALL, start_row)
    start_row = jnp.where(start_row >= BOX_ALL, start_row - BOX_ALL, start_row)
    start_row = jnp.minimum(start_row, 127)
    spread = jnp.where(
        lax.shift_right_logical(lane_o, 3) == sub_o, jnp.broadcast_to(start_row, (32, FRAME)), 0
    ).astype(F32).astype(BF)
    starts[...] = jnp.dot(spread, by_fun, preferred_element_type=F32).astype(jnp.int32) + jnp.bitwise_and(
        lane_o, SUP - 1
    )

    arrived = set()

    def wait_piece(ys, q):
        if (ys, q) in arrived:
            return
        arrived.add((ys, q))
        piece = frame.at[pl.ds(LEFT + FUN * ys, FUN), q]
        pltpu.make_async_copy(piece, piece, y_recv.at[ys, q]).wait()

    forwards = []
    for n, (ys, q, first, count, to) in enumerate(FORWARD):
        wait_piece(ys, q)
        src = LEFT + FUN * ys + first
        copy = pltpu.make_async_remote_copy(
            src_ref=frame.at[pl.ds(src, count), q],
            dst_ref=frame.at[pl.ds(src - OWN * to, count), q],
            send_sem=x_send.at[n],
            recv_sem=x_recv.at[n],
            device_id=dev(me + RING * to),
            device_id_type=MESH,
        )
        copy.start()
        forwards.append(copy)

    def pairs(step_of, first, count, width):
        def several(step, carry):
            for k in range(width):
                step_of(first + width * step + k, carry)
            return carry

        lax.fori_loop(0, count // width, several, 0)

    def into_slots(pair, carry):
        parts = []
        for half in range(2):
            octet = 2 * pair + half
            select = (row_id == meta[pl.ds(octet, 1), :]).astype(F32).astype(BF)
            raw = frame[pl.ds(pl.multiple_of(8 * octet, 8), 8)]
            raw = raw.astype(F32).reshape(FRAME, SLICE).astype(BF)
            out = jnp.dot(select, raw, preferred_element_type=F32)
            parts.append(out.reshape(SUP, 8, SLICE))
        both = jnp.concatenate(parts, axis=1).astype(BF)
        slots[:, pl.ds(pl.multiple_of(16 * pair, 16), 16), :] = both
        return carry

    for copy in forwards:
        copy.wait_recv()
    pairs(into_slots, 1, 4, W_HALO)
    pairs(into_slots, 11, 4, W_HALO)
    for ys in range(RING):
        for q in range(4):
            wait_piece(ys, q)

    loads[1].wait()
    potb[0:BOX, :] = pot[...].astype(BF)
    potb[BOX:16, :] = jnp.zeros((16 - BOX, 1024), BF)
    v_copies = []
    for o in range(-2, 5):
        if o == 0:
            copy = pltpu.make_async_copy(potb, v_win.at[2], v_recv.at[2])
        else:
            copy = pltpu.make_async_remote_copy(
                src_ref=potb,
                dst_ref=v_win.at[o + 2],
                send_sem=v_send.at[o + 2],
                recv_sem=v_recv.at[o + 2],
                device_id=dev(me - o),
                device_id_type=MESH,
            )
        copy.start()
        v_copies.append(copy)

    pairs(into_slots, 5, 6, W_OWN)

    def same_box(slot):
        box_row = rel_row + jnp.bitwise_and(slot - rel_row, SUP - 1)
        owned = jnp.logical_and(box_row >= low_row, box_row <= top_row)
        box_row = jnp.where(owned, box_row, -1)
        col = boxes[...]
        box_col = col + jnp.bitwise_and(slot - col, SUP - 1)
        return box_col == box_row[:, 0:128], box_col == box_row[:, 128:256]

    gram[...] = jnp.zeros((FRAME, FRAME), F32)

    def gram_step(step, carry):
        lo, hi = gram[:, 0:128], gram[:, 128:256]
        for part in range(4):
            slot = 4 * step + part
            held = slots[slot]
            prod = lax.dot_general(held, held, (((1,), (1,)), ((), ())), preferred_element_type=F32)
            same_lo, same_hi = same_box(slot)
            lo = lo + jnp.where(same_lo, prod[:, 0:128], 0.0)
            hi = hi + jnp.where(same_hi, prod[:, 128:256], 0.0)
        gram[:, 0:128] = lo
        gram[:, 128:256] = hi
        return carry

    lax.fori_loop(0, SUP // 4, gram_step, 0)
    scaled = gram[...] * VOLUME
    gram[...] = scaled
    high_part = scaled.astype(BF)
    rest = scaled - high_part.astype(F32)
    rest = jnp.sum(jnp.where(row_id == col_id, rest, 0.0), axis=1, keepdims=True)
    travels = jnp.where(col_id == FRAME - 1, rest, scaled)
    gram_out_rows[...] = travels.reshape(FRAME // 8, 8, FRAME).astype(BF)

    s_copies = []

    def send_terms(n, start, slot, target):
        copy = pltpu.make_async_remote_copy(
            src_ref=gram_out_rows.at[pl.ds(start, FUN // 8)],
            dst_ref=terms.at[slot],
            send_sem=s_send.at[n],
            recv_sem=s_recv.at[slot],
            device_id=dev(target),
            device_id_type=MESH,
        )
        copy.start()
        s_copies.append(copy)

    for yp in range(1, 4):
        send_terms(2 + yp, 3 * yp - 2, 8 + y, base - RING + yp)
    for yp in range(0, 3):
        send_terms(6 + yp, 22 + 3 * yp, y, base + RING + yp)
    for k in range(1, 4):
        yp = lax.rem(y + k, RING)
        send_terms(k - 1, LEFT // 8 + 3 * yp, 4 + y, base + yp)

    for copy in v_copies:
        if copy is v_copies[2]:
            copy.wait()
        else:
            copy.wait_recv()
    for k in range(7):
        pot_rows[BOX * k : BOX * k + BOX, :] = v_win[k].astype(F32)[0:BOX]
    pot_rows[7 * BOX : 128, :] = jnp.zeros((128 - 7 * BOX, 1024), F32)

    near_rows = pot_rows[...].astype(BF)
    row_of = lax.broadcasted_iota(jnp.int32, (128, FRAME), 0)
    for j in range(3):
        select = (row_of == starts[pl.ds(LEFT // 8 + 3 * y + j, 1), :]).astype(F32).astype(BF)
        local = lax.dot_general(select, near_rows, (((0,), (0,)), ((), ())), preferred_element_type=F32)
        pot_own[8 * j : 8 * j + 8] = local.reshape(8, 4, 8, 1024)

    def wait_terms(slot):
        pltpu.make_async_copy(terms.at[slot], terms.at[slot], s_recv.at[slot]).wait()

    def arrived_terms(slot):
        return terms[slot].astype(F32).reshape(FUN, FRAME)

    sums[0] = jnp.zeros((FUN, FRAME), F32)
    sums[2] = jnp.zeros((FUN, FRAME), F32)
    sums[1] = gram[my_rows, :]
    for k in range(1, 4):
        slot = 4 + lax.rem(y + k, RING)
        wait_terms(slot)
        sums[1] += arrived_terms(slot)

    @pl.when(y <= 2)
    def _():
        for ys in range(RING):
            wait_terms(ys)
        sums[0] = arrived_terms(0) + arrived_terms(1) + arrived_terms(2) + arrived_terms(3)

    @pl.when(y >= 1)
    def _():
        for ys in range(RING):
            wait_terms(8 + ys)
        sums[2] = arrived_terms(8) + arrived_terms(9) + arrived_terms(10) + arrived_terms(11)

    short_lane = lax.broadcasted_iota(jnp.int32, (FUN, FRAME), 1)
    short_sub = lax.broadcasted_iota(jnp.int32, (FUN, FRAME), 0)
    for n, at in enumerate((176, LEFT, -16)):
        held = sums[n]
        low_part = held[:, FRAME - 1 : FRAME]
        held = held + jnp.where(short_lane == short_sub + (FUN * y + at), low_part, 0.0)
        sums[n] = jnp.where(short_lane == FRAME - 1, 0.0, held)

    pad = jnp.zeros((FUN, FRAME), F32)
    wide = jnp.concatenate([sums[0], pad], axis=1)
    wide += pltpu.roll(jnp.concatenate([sums[1], pad], axis=1), 96, 1)
    wide += pltpu.roll(jnp.concatenate([sums[2], pad], axis=1), 192, 1)
    lane = lax.broadcasted_iota(jnp.int32, (FUN, 512), 1)
    sub = lax.broadcasted_iota(jnp.int32, (FUN, 512), 0)
    fixed = (1.5 * (lane == sub + (FUN * y + 176)).astype(F32) - 0.5 * wide)
    rows_out[0] = fixed[:, 0:256].astype(BF)
    rows_out[1] = pltpu.roll(fixed, 512 - 96, 1)[:, 0:256].astype(BF)
    rows_out[2] = pltpu.roll(fixed, 512 - 192, 1)[:, 0:256].astype(BF)

    c_copies = []

    def send_rows(n, which, slot, target):
        copy = pltpu.make_async_remote_copy(
            src_ref=rows_out.at[which],
            dst_ref=rows_in.at[slot],
            send_sem=c_send.at[n],
            recv_sem=c_recv.at[slot],
            device_id=dev(target),
            device_id_type=MESH,
        )
        copy.start()
        return copy

    own_rows = [
        send_rows(k - 1, 1, 4 + y, base + lax.rem(y + k, RING)) for k in range(1, 4)
    ]

    @pl.when(y <= 2)
    def _():
        for yp in range(RING):
            send_rows(3 + yp, 0, 8 + y, base - RING + yp)

    @pl.when(y >= 1)
    def _():
        for yp in range(RING):
            send_rows(7 + yp, 2, y, base + RING + yp)

    band = pltpu.roll(wide, 512 - 49 - FUN * y, 1)
    for bit in range(5):
        moved = pltpu.roll(band, 512 - (1 << bit), 1)
        band = jnp.where(jnp.bitwise_and(sub, 1 << bit) != 0, moved, band)
    gram_out[...] = jnp.where(lane[:, 0:256] == 255, 0.0, band[:, 0:256])
    gram_copy = pltpu.make_async_copy(gram_out, gram_hbm, kin_sem.at[3])
    gram_copy.start()

    def wait_rows(slot):
        pltpu.make_async_copy(rows_in.at[slot], rows_in.at[slot], c_recv.at[slot]).wait()

    mixing[0:16, :] = jnp.zeros((16, FRAME), F32)
    mixing[240:256, :] = jnp.zeros((16, FRAME), F32)
    mixing[my_rows, :] = rows_out[1].astype(F32)
    for k in range(1, 4):
        ys = lax.rem(y + k, RING)
        wait_rows(4 + ys)
        mixing[pl.ds(pl.multiple_of(LEFT + FUN * ys, 8), FUN), :] = rows_in[4 + ys].astype(F32)
    for ys in range(0, 3):
        wait_rows(8 + ys)
        mixing[176 + FUN * ys : 200 + FUN * ys, :] = rows_in[8 + ys].astype(F32)
    for ys in range(1, 4):
        wait_rows(ys)
        mixing[FUN * ys - 16 : FUN * ys + 8, :] = rows_in[ys].astype(F32)

    def mix_step(step, carry):
        for part in range(4):
            slot = 4 * step + part
            same_lo, same_hi = same_box(slot)
            mix = jnp.concatenate(
                [jnp.where(same_lo, mixing[:, 0:128], 0.0), jnp.where(same_hi, mixing[:, 128:256], 0.0)], axis=1
            ).astype(BF)
            slots[slot] = jnp.dot(mix, slots[slot], preferred_element_type=F32).astype(BF)
        return carry

    lax.fori_loop(0, SUP // 4, mix_step, 0)

    for copy in forwards:
        copy.wait_send()

    def out_of_slots(pair, carry):
        both = slots[:, pl.ds(pl.multiple_of(16 * pair, 16), 16), :].astype(F32)
        for half in range(2):
            octet = 2 * pair + half
            select = (row_id == meta[pl.ds(32 + octet, 1), :]).astype(F32).astype(BF)
            part = both[:, 8 * half : 8 * half + 8, :].reshape(FRAME, SLICE).astype(BF)
            out = jnp.dot(select, part, preferred_element_type=F32)
            frame[pl.ds(pl.multiple_of(8 * octet, 8), 8)] = out.reshape(8, 4, 8, SLICE).astype(BF)
        return carry

    backs = (back_a, back_b, back_c, back_d)
    x_backs = []
    for n, (src, q, nq, dst, to) in enumerate(HALO):
        pairs(out_of_slots, dst // 16, 2, 2)
        copy = pltpu.make_async_remote_copy(
            src_ref=frame.at[pl.ds(dst, 32), pl.ds(q, nq)],
            dst_ref=backs[n],
            send_sem=bx_send.at[n],
            recv_sem=bx_recv.at[n],
            device_id=dev(me - RING * to),
            device_id_type=MESH,
        )
        copy.start()
        x_backs.append(copy)
    pairs(out_of_slots, 5, 6, W_OWN)

    lanes = pl.ds(pl.multiple_of(y * SLICE, SLICE), SLICE)
    y_backs = []

    def quarters(octet):
        unit = lax.div(octet, 4)
        clean = 2 - unit
        first = 2 * lax.div(unit, 2)
        second = 3 - 2 * lax.div(3 - unit, 3)
        return ((clean, 2),), ((first, 1), (second, 1))

    def send_home(which):
        for k in (1, 3, 2, 0):
            yp = lax.rem(y + k, RING)
            for j in range(3):
                for n, (q, nq) in enumerate(quarters(3 * yp + j)[which]):
                    src = frame.at[pl.ds(pl.multiple_of(LEFT + FUN * yp + 8 * j, 8), 8), pl.ds(q, nq)]
                    dst = y_in.at[pl.ds(8 * j, 8), pl.ds(q, nq), :, lanes]
                    if k == 0:
                        pltpu.make_async_copy(src, dst, by_recv.at[y, j, which + n]).start()
                        continue
                    copy = pltpu.make_async_remote_copy(
                        src_ref=src,
                        dst_ref=dst,
                        send_sem=by_send.at[k - 1, j, which + n],
                        recv_sem=by_recv.at[y, j, which + n],
                        device_id=dev(base + yp),
                        device_id_type=MESH,
                    )
                    copy.start()
                    y_backs.append(copy)

    send_home(0)
    for n, (src, q, nq, dst, to) in enumerate(HALO):
        x_backs[n].wait_recv()
        mine = frame[src : src + 32, q : q + nq].astype(F32)
        frame[src : src + 32, q : q + nq] = (mine + backs[n][...].astype(F32)).astype(BF)
    send_home(1)

    loads[2].wait()
    out_copies = []
    for which in range(2):
        for j in range(3):
            octs = quarters(3 * y + j)[which]
            for n, (q, nq) in enumerate(octs):
                for ys in range(RING):
                    part = y_in.at[pl.ds(8 * j, 8), pl.ds(q, nq), :, pl.ds(ys * SLICE, SLICE)]
                    pltpu.make_async_copy(part, part, by_recv.at[ys, j, which + n]).wait()
                rows = 8 * 8 * nq
                at = 128 * j + rows * n
                piece = y_in[8 * j : 8 * j + 8, pl.ds(q, nq)].astype(F32).reshape(rows, 1024)
                x_in[at : at + rows, :] = piece.astype(BF)
        for t in range(4):
            cols = slice(256 * t, 256 * t + 256)
            applied = jnp.dot(x_in[...], kin[:, cols], preferred_element_type=F32)
            for j in range(3):
                octs = quarters(3 * y + j)[which]
                for n, (q, nq) in enumerate(octs):
                    rows = 8 * 8 * nq
                    at = 128 * j + rows * n
                    local = pot_own[8 * j : 8 * j + 8, pl.ds(q, nq), :, cols].reshape(rows, 256)
                    res = applied[at : at + rows] + local * x_in[at : at + rows, cols].astype(F32)
                    y_res[8 * j : 8 * j + 8, pl.ds(q, nq), :, cols] = res.reshape(8, nq, 8, 256).astype(BF)
        for j in range(3):
            octs = quarters(3 * y + j)[which]
            for n, (q, nq) in enumerate(octs):
                copy = pltpu.make_async_copy(
                    y_res.at[pl.ds(8 * j, 8), pl.ds(q, nq)],
                    out.at[pl.ds(8 * j, 8), pl.ds(q, nq)],
                    out_sem.at[j, which + n],
                )
                copy.start()
                out_copies.append(copy)

    for copy in started:
        copy.wait_send()
    for k, copy in enumerate(v_copies):
        if k != 2:
            copy.wait_send()
    for copy in s_copies:
        copy.wait_send()
    for copy in own_rows:
        copy.wait_send()

    @pl.when(y <= 2)
    def _():
        for yp in range(RING):
            pltpu.make_async_copy(rows_out.at[0], rows_out.at[0], c_send.at[3 + yp]).wait()

    @pl.when(y >= 1)
    def _():
        for yp in range(RING):
            pltpu.make_async_copy(rows_out.at[2], rows_out.at[2], c_send.at[7 + yp]).wait()

    for copy in x_backs:
        copy.wait_send()
    for copy in y_backs:
        copy.wait_send()
    for copy in out_copies:
        copy.wait()
    gram_copy.wait()


def on_device(coeffs, centers, kinetic, potential):
    hbm = pl.BlockSpec(memory_space=pl.ANY)
    dma = pltpu.SemaphoreType.DMA
    filtered, gram_band = pl.pallas_call(
        exchange_kernel,
        out_shape=(
            jax.ShapeDtypeStruct((FUN, 4, 8, 1024), BF),
            jax.ShapeDtypeStruct((FUN, FRAME), F32),
        ),
        in_specs=[hbm, hbm, hbm, hbm],
        out_specs=(hbm, hbm),
        scratch_shapes=[
            pltpu.VMEM((FRAME, 4, 8, SLICE), BF),
            pltpu.VMEM((SUP, FRAME, SLICE), BF),
            pltpu.VMEM((FRAME // 8, 8, FRAME), BF),
            pltpu.VMEM((32, 2, 8, SLICE), BF),
            pltpu.VMEM((32, 2, 8, SLICE), BF),
            pltpu.VMEM((32, 1, 8, SLICE), BF),
            pltpu.VMEM((32, 1, 8, SLICE), BF),
            pltpu.VMEM((FRAME, FRAME), F32),
            pltpu.VMEM((12, FUN // 8, 8, FRAME), BF),
            pltpu.VMEM((3, FUN, FRAME), F32),
            pltpu.VMEM((3, FUN, FRAME), BF),
            pltpu.VMEM((12, FUN, FRAME), BF),
            pltpu.VMEM((FRAME, FRAME), F32),
            pltpu.VMEM((16, 1024), BF),
            pltpu.VMEM((FRAME, 128), jnp.int32),
            pltpu.VMEM((BOX, 1024), F32),
            pltpu.VMEM((FUN, 128), jnp.int32),
            pltpu.VMEM((FUN, FRAME), F32),
            pltpu.VMEM((64, FRAME), jnp.int32),
            pltpu.VMEM((32, FRAME), jnp.int32),
            pltpu.VMEM((1024, 1024), BF),
            pltpu.VMEM((7, 16, 1024), BF),
            pltpu.VMEM((128, 1024), F32),
            pltpu.VMEM((FUN, 4, 8, 1024), F32),
            pltpu.VMEM((FUN, 4, 8, 1024), BF),
            pltpu.VMEM((384, 1024), BF),
            pltpu.VMEM((FUN, 4, 8, 1024), BF),
            dma((3, 4)), dma((4, 4)), dma((10,)), dma((10,)), dma((7,)), dma((7,)),
            dma((9,)), dma((12,)), dma((11,)), dma((12,)), dma((4,)), dma((4,)),
            dma((3, 3, 3)), dma((4, 3, 3)), dma((4,)), dma((3, 3)),
        ],
        compiler_params=pltpu.CompilerParams(collective_id=0, has_side_effects=True),
        name="exchange",
    )(coeffs.reshape(FUN, 4, 8, 1024), kinetic, potential, centers.reshape(FUN, 128))
    return filtered.reshape(FUN, SUP, 1024), gram_band


def solution(mesh):
    placed = (P(("func", "box"), None, None), P(), P(), P(("func", "box"), None))
    return jax.shard_map(
        on_device,
        mesh=mesh,
        in_specs=placed,
        out_specs=(P(("func", "box"), None, None), P(("func", "box"), None)),
        check_vma=False,
    )
```

```python
import jax
import jax.numpy as jnp
from jax import lax
from jax.experimental import pallas as pl
from jax.experimental.pallas import tpu as pltpu
from jax.sharding import PartitionSpec as P

MESH = pl.DeviceIdType.MESH
BF = jnp.bfloat16
F32 = jnp.float32

SUP = 32
FUN = 24
BOX = 12
RING = 4
OWN = FUN * RING
FRAME = 256
LEFT = 80
SLICE = 256
BOX_ALL = 1536
FUN_ALL = 3072
W_HALO = 4
W_OWN = 6
VOLUME = 1.0 / (32 * 1024)

HALO = (
    (80, 0, 2, 176, -1),
    (144, 2, 2, 48, 1),
    (112, 0, 1, 208, -1),
    (112, 3, 1, 16, 1),
)
FORWARD = (
    (0, 0, 0, 24, -1),
    (3, 3, 0, 24, 1),
    (1, 0, 0, 24, -1),
    (2, 3, 0, 24, 1),
    (0, 1, 0, 24, -1),
    (3, 2, 0, 24, 1),
    (2, 0, 0, 16, -1),
    (1, 3, 8, 16, 1),
    (1, 1, 0, 8, -1),
    (2, 2, 16, 8, 1),
)


def exchange_kernel(
    coeffs, kinetic, pot_hbm, lanes_hbm, y_res, gram_out,
    frame, slots, gram_out_rows, back_a, back_b, back_c, back_d, gram, terms, sums, rows_out, rows_in, mixing, potb, boxes,
    pot, lanes_in, meta, starts, kin, v_win, pot_rows, pot_own, y_in, x_in,
    y_send, y_recv, x_send, x_recv, v_send, v_recv, s_send, s_recv, c_send, c_recv, bx_send, bx_recv,
    by_send, by_recv, kin_sem,
):
    me = lax.axis_index("func") * 16 + lax.axis_index("box")
    y = lax.rem(me, RING)
    base = me - y

    def dev(linear):
        wrapped = lax.rem(linear + 128, 128)
        return (lax.div(wrapped, 16), lax.rem(wrapped, 16))

    barrier = pltpu.get_barrier_semaphore()
    partners = [base + lax.rem(y + k, RING) for k in range(1, RING)] + [me + RING, me - RING]
    for partner in partners:
        pl.semaphore_signal(barrier, inc=1, device_id=dev(partner), device_id_type=MESH)

    loads = [
        pltpu.make_async_copy(src, dst, kin_sem.at[n])
        for n, (src, dst) in enumerate(((lanes_hbm, lanes_in), (pot_hbm, pot), (kinetic, kin)))
    ]
    for copy in loads:
        copy.start()

    pl.semaphore_wait(barrier, len(partners))

    started = []

    my_rows = pl.ds(pl.multiple_of(LEFT + FUN * y, 8), FUN)
    high = lax.div(y, 2)
    inner = lax.rem(lax.div(y + 1, 2), 2)

    for p in range(4):
        q0 = p + inner * ((0, 3, 1, 2)[p] - p)
        q = q0 + high * (3 - 2 * q0)
        for k in (1, 3, 2):
            yp = lax.rem(y + k, RING)
            copy = pltpu.make_async_remote_copy(
                src_ref=coeffs.at[:, q, :, pl.ds(pl.multiple_of(yp * SLICE, SLICE), SLICE)],
                dst_ref=frame.at[my_rows, q],
                send_sem=y_send.at[k - 1, p],
                recv_sem=y_recv.at[y, q],
                device_id=dev(base + yp),
                device_id_type=MESH,
            )
            copy.start()
            started.append(copy)
        pltpu.make_async_copy(
            coeffs.at[:, q, :, pl.ds(pl.multiple_of(y * SLICE, SLICE), SLICE)],
            frame.at[my_rows, q],
            y_recv.at[y, q],
        ).start()

    frame[16:48, 0:3] = jnp.zeros((32, 3, 8, SLICE), BF)
    frame[48:80, 0:2] = jnp.zeros((32, 2, 8, SLICE), BF)
    frame[176:208, 2:4] = jnp.zeros((32, 2, 8, SLICE), BF)
    frame[208:240, 1:4] = jnp.zeros((32, 3, 8, SLICE), BF)
    slots[:, 0:16, :] = jnp.zeros((SUP, 16, SLICE), BF)
    slots[:, 240:256, :] = jnp.zeros((SUP, 16, SLICE), BF)

    loads[0].wait()
    ring = lax.div(me, RING)
    flat = ring * OWN - LEFT + FUN_ALL
    top_line = lax.div(flat, 128)
    lines = [lanes_in[pl.ds(lax.rem(top_line + k, FUN_ALL // 128), 1), :] for k in range(3)]
    near = pltpu.roll(jnp.concatenate(lines, axis=1), 384 - lax.rem(flat, 128), 1)[:, 0:FRAME]
    row_lane = lax.broadcasted_iota(jnp.int32, (1, FRAME), 1)

    def pick(row, lane_at):
        return jnp.sum(jnp.where(row_lane == lane_at, row, 0), axis=1, keepdims=True)

    rel_row = near - pick(near, LEFT) + OWN
    rel_row = jnp.where(rel_row < 0, rel_row + BOX_ALL, rel_row)
    rel_row = jnp.where(rel_row >= BOX_ALL, rel_row - BOX_ALL, rel_row)
    low_row = OWN + 16
    top_row = pick(rel_row, LEFT + OWN - 1) + 16
    row_id = lax.broadcasted_iota(jnp.int32, (FRAME, FRAME), 0)
    col_id = lax.broadcasted_iota(jnp.int32, (FRAME, FRAME), 1)
    rel_tile = jnp.broadcast_to(rel_row, (FRAME, FRAME))
    rel_col = jnp.sum(
        jnp.where(row_id == col_id, rel_tile.astype(F32), 0.0), axis=1, keepdims=True
    ).astype(jnp.int32)
    boxes[...] = jnp.broadcast_to(rel_col, (FRAME, 128))
    sub_o = lax.broadcasted_iota(jnp.int32, (32, FRAME), 0)
    lane_o = lax.broadcasted_iota(jnp.int32, (32, FRAME), 1)
    rest_row = jnp.bitwise_and(rel_row, SUP - 1)
    spread = jnp.where(
        lax.shift_right_logical(lane_o, 3) == sub_o, jnp.broadcast_to(rest_row, (32, FRAME)), 0
    ).astype(F32).astype(BF)
    in_octet = jnp.bitwise_and(row_id, 7)
    by_fun = (in_octet == lax.shift_right_logical(col_id, 5)).astype(F32).astype(BF)
    by_low = (in_octet == jnp.bitwise_and(col_id, 7)).astype(F32).astype(BF)
    rest_fun = jnp.dot(spread, by_fun, preferred_element_type=F32).astype(jnp.int32)
    rest_low = jnp.dot(spread, by_low, preferred_element_type=F32).astype(jnp.int32)
    meta[0:32, :] = jnp.bitwise_and(rest_fun + lane_o, SUP - 1) * 8 + lax.shift_right_logical(lane_o, 5)
    meta[32:64, :] = jnp.bitwise_and(lane_o, 7) * SUP + jnp.bitwise_and(
        lax.shift_right_logical(lane_o, 3) - rest_low, SUP - 1
    )

    start_row = near - BOX * (me - 2)
    start_row = jnp.where(start_row < 0, start_row + BOX_ALL, start_row)
    start_row = jnp.where(start_row >= BOX_ALL, start_row - BOX_ALL, start_row)
    start_row = jnp.minimum(start_row, 127)
    spread = jnp.where(
        lax.shift_right_logical(lane_o, 3) == sub_o, jnp.broadcast_to(start_row, (32, FRAME)), 0
    ).astype(F32).astype(BF)
    starts[...] = jnp.dot(spread, by_fun, preferred_element_type=F32).astype(jnp.int32) + jnp.bitwise_and(
        lane_o, SUP - 1
    )

    arrived = set()

    def wait_piece(ys, q):
        if (ys, q) in arrived:
            return
        arrived.add((ys, q))
        piece = frame.at[pl.ds(LEFT + FUN * ys, FUN), q]
        pltpu.make_async_copy(piece, piece, y_recv.at[ys, q]).wait()

    forwards = []
    for n, (ys, q, first, count, to) in enumerate(FORWARD):
        wait_piece(ys, q)
        src = LEFT + FUN * ys + first
        copy = pltpu.make_async_remote_copy(
            src_ref=frame.at[pl.ds(src, count), q],
            dst_ref=frame.at[pl.ds(src - OWN * to, count), q],
            send_sem=x_send.at[n],
            recv_sem=x_recv.at[n],
            device_id=dev(me + RING * to),
            device_id_type=MESH,
        )
        copy.start()
        forwards.append(copy)

    def pairs(step_of, first, count, width):
        def several(step, carry):
            for k in range(width):
                step_of(first + width * step + k, carry)
            return carry

        lax.fori_loop(0, count // width, several, 0)

    def into_slots(pair, carry):
        parts = []
        for half in range(2):
            octet = 2 * pair + half
            select = (row_id == meta[pl.ds(octet, 1), :]).astype(F32).astype(BF)
            raw = frame[pl.ds(pl.multiple_of(8 * octet, 8), 8)]
            raw = raw.astype(F32).reshape(FRAME, SLICE).astype(BF)
            out = jnp.dot(select, raw, preferred_element_type=F32)
            parts.append(out.reshape(SUP, 8, SLICE))
        both = jnp.concatenate(parts, axis=1).astype(BF)
        slots[:, pl.ds(pl.multiple_of(16 * pair, 16), 16), :] = both
        return carry

    for copy in forwards:
        copy.wait_recv()
    pairs(into_slots, 1, 4, W_HALO)
    pairs(into_slots, 11, 4, W_HALO)
    for ys in range(RING):
        for q in range(4):
            wait_piece(ys, q)

    loads[1].wait()
    potb[0:BOX, :] = pot[...].astype(BF)
    potb[BOX:16, :] = jnp.zeros((16 - BOX, 1024), BF)
    v_copies = []
    for o in range(-2, 5):
        if o == 0:
            copy = pltpu.make_async_copy(potb, v_win.at[2], v_recv.at[2])
        else:
            copy = pltpu.make_async_remote_copy(
                src_ref=potb,
                dst_ref=v_win.at[o + 2],
                send_sem=v_send.at[o + 2],
                recv_sem=v_recv.at[o + 2],
                device_id=dev(me - o),
                device_id_type=MESH,
            )
        copy.start()
        v_copies.append(copy)

    pairs(into_slots, 5, 6, W_OWN)

    def same_box(slot):
        box_row = rel_row + jnp.bitwise_and(slot - rel_row, SUP - 1)
        owned = jnp.logical_and(box_row >= low_row, box_row <= top_row)
        box_row = jnp.where(owned, box_row, -1)
        col = boxes[...]
        box_col = col + jnp.bitwise_and(slot - col, SUP - 1)
        return box_col == box_row[:, 0:128], box_col == box_row[:, 128:256]

    gram[...] = jnp.zeros((FRAME, FRAME), F32)

    def gram_step(step, carry):
        lo, hi = gram[:, 0:128], gram[:, 128:256]
        for part in range(4):
            slot = 4 * step + part
            held = slots[slot]
            prod = lax.dot_general(held, held, (((1,), (1,)), ((), ())), preferred_element_type=F32)
            same_lo, same_hi = same_box(slot)
            lo = lo + jnp.where(same_lo, prod[:, 0:128], 0.0)
            hi = hi + jnp.where(same_hi, prod[:, 128:256], 0.0)
        gram[:, 0:128] = lo
        gram[:, 128:256] = hi
        return carry

    lax.fori_loop(0, SUP // 4, gram_step, 0)
    scaled = gram[...] * VOLUME
    gram[...] = scaled
    high_part = scaled.astype(BF)
    rest = scaled - high_part.astype(F32)
    rest = jnp.sum(jnp.where(row_id == col_id, rest, 0.0), axis=1, keepdims=True)
    travels = jnp.where(col_id == FRAME - 1, rest, scaled)
    gram_out_rows[...] = travels.reshape(FRAME // 8, 8, FRAME).astype(BF)

    s_copies = []

    def send_terms(n, start, slot, target):
        copy = pltpu.make_async_remote_copy(
            src_ref=gram_out_rows.at[pl.ds(start, FUN // 8)],
            dst_ref=terms.at[slot],
            send_sem=s_send.at[n],
            recv_sem=s_recv.at[slot],
            device_id=dev(target),
            device_id_type=MESH,
        )
        copy.start()
        s_copies.append(copy)

    for yp in range(1, 4):
        send_terms(2 + yp, 3 * yp - 2, 8 + y, base - RING + yp)
    for yp in range(0, 3):
        send_terms(6 + yp, 22 + 3 * yp, y, base + RING + yp)
    for k in range(1, 4):
        yp = lax.rem(y + k, RING)
        send_terms(k - 1, LEFT // 8 + 3 * yp, 4 + y, base + yp)

    for copy in v_copies:
        if copy is v_copies[2]:
            copy.wait()
        else:
            copy.wait_recv()
    for k in range(7):
        pot_rows[BOX * k : BOX * k + BOX, :] = v_win[k].astype(F32)[0:BOX]
    pot_rows[7 * BOX : 128, :] = jnp.zeros((128 - 7 * BOX, 1024), F32)

    near_rows = pot_rows[...].astype(BF)
    row_of = lax.broadcasted_iota(jnp.int32, (128, FRAME), 0)
    for j in range(3):
        select = (row_of == starts[pl.ds(LEFT // 8 + 3 * y + j, 1), :]).astype(F32).astype(BF)
        local = lax.dot_general(select, near_rows, (((0,), (0,)), ((), ())), preferred_element_type=F32)
        pot_own[8 * j : 8 * j + 8] = local.reshape(8, 4, 8, 1024)

    def wait_terms(slot):
        pltpu.make_async_copy(terms.at[slot], terms.at[slot], s_recv.at[slot]).wait()

    def arrived_terms(slot):
        return terms[slot].astype(F32).reshape(FUN, FRAME)

    sums[0] = jnp.zeros((FUN, FRAME), F32)
    sums[2] = jnp.zeros((FUN, FRAME), F32)
    sums[1] = gram[my_rows, :]
    for k in range(1, 4):
        slot = 4 + lax.rem(y + k, RING)
        wait_terms(slot)
        sums[1] += arrived_terms(slot)

    @pl.when(y <= 2)
    def _():
        for ys in range(RING):
            wait_terms(ys)
        sums[0] = arrived_terms(0) + arrived_terms(1) + arrived_terms(2) + arrived_terms(3)

    @pl.when(y >= 1)
    def _():
        for ys in range(RING):
            wait_terms(8 + ys)
        sums[2] = arrived_terms(8) + arrived_terms(9) + arrived_terms(10) + arrived_terms(11)

    short_lane = lax.broadcasted_iota(jnp.int32, (FUN, FRAME), 1)
    short_sub = lax.broadcasted_iota(jnp.int32, (FUN, FRAME), 0)
    for n, at in enumerate((176, LEFT, -16)):
        held = sums[n]
        low_part = held[:, FRAME - 1 : FRAME]
        held = held + jnp.where(short_lane == short_sub + (FUN * y + at), low_part, 0.0)
        sums[n] = jnp.where(short_lane == FRAME - 1, 0.0, held)

    pad = jnp.zeros((FUN, FRAME), F32)
    wide = jnp.concatenate([sums[0], pad], axis=1)
    wide += pltpu.roll(jnp.concatenate([sums[1], pad], axis=1), 96, 1)
    wide += pltpu.roll(jnp.concatenate([sums[2], pad], axis=1), 192, 1)
    lane = lax.broadcasted_iota(jnp.int32, (FUN, 512), 1)
    sub = lax.broadcasted_iota(jnp.int32, (FUN, 512), 0)
    fixed = (1.5 * (lane == sub + (FUN * y + 176)).astype(F32) - 0.5 * wide)
    rows_out[0] = fixed[:, 0:256].astype(BF)
    rows_out[1] = pltpu.roll(fixed, 512 - 96, 1)[:, 0:256].astype(BF)
    rows_out[2] = pltpu.roll(fixed, 512 - 192, 1)[:, 0:256].astype(BF)

    c_copies = []

    def send_rows(n, which, slot, target):
        copy = pltpu.make_async_remote_copy(
            src_ref=rows_out.at[which],
            dst_ref=rows_in.at[slot],
            send_sem=c_send.at[n],
            recv_sem=c_recv.at[slot],
            device_id=dev(target),
            device_id_type=MESH,
        )
        copy.start()
        return copy

    @pl.when(y <= 2)
    def _():
        for yp in range(RING):
            send_rows(3 + yp, 0, 8 + y, base - RING + yp)

    @pl.when(y >= 1)
    def _():
        for yp in range(RING):
            send_rows(7 + yp, 2, y, base + RING + yp)

    own_rows = [
        send_rows(k - 1, 1, 4 + y, base + lax.rem(y + k, RING)) for k in range(1, 4)
    ]

    band = pltpu.roll(wide, 512 - 49 - FUN * y, 1)
    for bit in range(5):
        moved = pltpu.roll(band, 512 - (1 << bit), 1)
        band = jnp.where(jnp.bitwise_and(sub, 1 << bit) != 0, moved, band)
    gram_out[...] = jnp.where(lane[:, 0:256] == 255, 0.0, band[:, 0:256])

    def wait_rows(slot):
        pltpu.make_async_copy(rows_in.at[slot], rows_in.at[slot], c_recv.at[slot]).wait()

    mixing[0:16, :] = jnp.zeros((16, FRAME), F32)
    mixing[240:256, :] = jnp.zeros((16, FRAME), F32)
    mixing[my_rows, :] = rows_out[1].astype(F32)
    for k in range(1, 4):
        ys = lax.rem(y + k, RING)
        wait_rows(4 + ys)
        mixing[pl.ds(pl.multiple_of(LEFT + FUN * ys, 8), FUN), :] = rows_in[4 + ys].astype(F32)
    for ys in range(0, 3):
        wait_rows(8 + ys)
        mixing[176 + FUN * ys : 200 + FUN * ys, :] = rows_in[8 + ys].astype(F32)
    for ys in range(1, 4):
        wait_rows(ys)
        mixing[FUN * ys - 16 : FUN * ys + 8, :] = rows_in[ys].astype(F32)

    def mix_step(step, carry):
        for part in range(4):
            slot = 4 * step + part
            same_lo, same_hi = same_box(slot)
            mix = jnp.concatenate(
                [jnp.where(same_lo, mixing[:, 0:128], 0.0), jnp.where(same_hi, mixing[:, 128:256], 0.0)], axis=1
            ).astype(BF)
            slots[slot] = jnp.dot(mix, slots[slot], preferred_element_type=F32).astype(BF)
        return carry

    lax.fori_loop(0, SUP // 4, mix_step, 0)

    for copy in forwards:
        copy.wait_send()

    def out_of_slots(pair, carry):
        both = slots[:, pl.ds(pl.multiple_of(16 * pair, 16), 16), :].astype(F32)
        for half in range(2):
            octet = 2 * pair + half
            select = (row_id == meta[pl.ds(32 + octet, 1), :]).astype(F32).astype(BF)
            part = both[:, 8 * half : 8 * half + 8, :].reshape(FRAME, SLICE).astype(BF)
            out = jnp.dot(select, part, preferred_element_type=F32)
            frame[pl.ds(pl.multiple_of(8 * octet, 8), 8)] = out.reshape(8, 4, 8, SLICE).astype(BF)
        return carry

    backs = (back_a, back_b, back_c, back_d)
    x_backs = []
    lanes = pl.ds(pl.multiple_of(y * SLICE, SLICE), SLICE)

    def halo_back(n):
        src, q, nq, dst, to = HALO[n]
        pairs(out_of_slots, dst // 16, 2, 2)
        copy = pltpu.make_async_remote_copy(
            src_ref=frame.at[pl.ds(dst, 32), pl.ds(q, nq)],
            dst_ref=backs[n],
            send_sem=bx_send.at[n],
            recv_sem=bx_recv.at[n],
            device_id=dev(me - RING * to),
            device_id_type=MESH,
        )
        copy.start()
        x_backs.append(copy)

    def merge(n):
        src, q, nq, dst, to = HALO[n]
        x_backs[n].wait_recv()
        mine = frame[src : src + 32, q : q + nq].astype(F32)
        frame[src : src + 32, q : q + nq] = (mine + backs[n][...].astype(F32)).astype(BF)

    def quarters(octet):
        unit = octet // 4 if isinstance(octet, int) else lax.div(octet, 4)
        half = (unit + 1) // 3 if isinstance(octet, int) else lax.div(unit + 1, 3)
        late = (unit + 2) // 3 if isinstance(octet, int) else lax.div(unit + 2, 3)
        return ((2 - unit, 2),), ((2 * half, 1), (1 + 2 * late, 1))

    def home_part(octet, n, which):
        q, nq = quarters(octet)[which][n]
        return frame.at[pl.ds(LEFT + 8 * octet, 8), pl.ds(q, nq)]

    def send_home(octets, which):
        for octet in octets:
            yp, j = octet // 3, octet % 3
            for n, (q, nq) in enumerate(quarters(octet)[which]):
                src = home_part(octet, n, which)
                dst = y_in.at[pl.ds(8 * j, 8), pl.ds(q, nq), :, lanes]
                kind = which + n

                @pl.when(y != yp)
                def _():
                    pltpu.make_async_remote_copy(
                        src_ref=src,
                        dst_ref=dst,
                        send_sem=by_send.at[octet, kind],
                        recv_sem=by_recv.at[y, j, kind],
                        device_id=dev(base + yp),
                        device_id_type=MESH,
                    ).start()

                @pl.when(y == yp)
                def _():
                    pltpu.make_async_copy(src, dst, by_recv.at[y, j, kind]).start()

    pairs(out_of_slots, 5, 3, 3)
    send_home(range(0, 6), 0)
    halo_back(0)
    halo_back(1)
    pairs(out_of_slots, 8, 3, 3)
    send_home(range(6, 12), 0)
    halo_back(2)
    halo_back(3)
    merge(0)
    send_home(range(0, 4), 1)
    merge(1)
    send_home(range(8, 12), 1)
    merge(2)
    merge(3)
    send_home(range(4, 8), 1)

    loads[2].wait()
    for which in range(2):
        for k in (0, 1, 3, 2):
            ys = lax.rem(y + k, RING)
            cols = pl.ds(pl.multiple_of(ys * SLICE, SLICE), SLICE)
            for j in range(3):
                for n, (q, nq) in enumerate(quarters(3 * y + j)[which]):
                    part = y_in.at[pl.ds(8 * j, 8), pl.ds(q, nq), :, cols]
                    pltpu.make_async_copy(part, part, by_recv.at[ys, j, which + n]).wait()
            held, local = [], []
            for j in range(3):
                for n, (q, nq) in enumerate(quarters(3 * y + j)[which]):
                    part = (slice(8 * j, 8 * j + 8), pl.ds(q, nq), slice(None), cols)
                    held.append(y_in[part].astype(F32).reshape(64 * nq, SLICE))
                    local.append(pot_own[part].reshape(64 * nq, SLICE))
            held = jnp.concatenate(held, axis=0)
            local = jnp.concatenate(local, axis=0)
            applied = jnp.dot(held.astype(BF), kin[cols, :], preferred_element_type=F32)
            if k == 0:
                x_in[...] = applied
            else:
                x_in[...] += applied
            x_in[:, cols] += local * held
        at = 0
        for j in range(3):
            for n, (q, nq) in enumerate(quarters(3 * y + j)[which]):
                piece = x_in[at : at + 64 * nq, :].astype(BF).astype(F32)
                y_res[8 * j : 8 * j + 8, pl.ds(q, nq)] = piece.reshape(8, nq, 8, 1024).astype(BF)
                at += 64 * nq

    for copy in started:
        copy.wait_send()
    for k, copy in enumerate(v_copies):
        if k != 2:
            copy.wait_send()
    for copy in s_copies:
        copy.wait_send()
    for copy in own_rows:
        copy.wait_send()

    @pl.when(y <= 2)
    def _():
        for yp in range(RING):
            pltpu.make_async_copy(rows_out.at[0], rows_out.at[0], c_send.at[3 + yp]).wait()

    @pl.when(y >= 1)
    def _():
        for yp in range(RING):
            pltpu.make_async_copy(rows_out.at[2], rows_out.at[2], c_send.at[7 + yp]).wait()

    for copy in x_backs:
        copy.wait_send()
    for octet in range(12):
        for which in range(2):
            for n in range(which + 1):
                part = home_part(octet, n, which)

                @pl.when(y != octet // 3)
                def _():
                    pltpu.make_async_copy(part, part, by_send.at[octet, which + n]).wait()


def write_kernel(pieces, rows, pieces_out, rows_out, sem):
    copies = [
        pltpu.make_async_copy(pieces, pieces_out, sem.at[0]),
        pltpu.make_async_copy(rows, rows_out, sem.at[1]),
    ]
    for copy in copies:
        copy.start()
    for copy in copies:
        copy.wait()


def on_device(coeffs, centers, kinetic, potential):
    hbm = pl.BlockSpec(memory_space=pl.ANY)
    vmem = pl.BlockSpec(memory_space=pltpu.VMEM)
    dma = pltpu.SemaphoreType.DMA
    results = pl.pallas_call(
        exchange_kernel,
        out_shape=(
            pltpu.VMEM((FUN, 4, 8, 1024), BF),
            pltpu.VMEM((FUN, FRAME), F32),
        ),
        in_specs=[hbm, hbm, hbm, hbm],
        out_specs=(vmem, vmem),
        scratch_shapes=[
            pltpu.VMEM((FRAME, 4, 8, SLICE), BF),
            pltpu.VMEM((SUP, FRAME, SLICE), BF),
            pltpu.VMEM((FRAME // 8, 8, FRAME), BF),
            pltpu.VMEM((32, 2, 8, SLICE), BF),
            pltpu.VMEM((32, 2, 8, SLICE), BF),
            pltpu.VMEM((32, 1, 8, SLICE), BF),
            pltpu.VMEM((32, 1, 8, SLICE), BF),
            pltpu.VMEM((FRAME, FRAME), F32),
            pltpu.VMEM((12, FUN // 8, 8, FRAME), BF),
            pltpu.VMEM((3, FUN, FRAME), F32),
            pltpu.VMEM((3, FUN, FRAME), BF),
            pltpu.VMEM((12, FUN, FRAME), BF),
            pltpu.VMEM((FRAME, FRAME), F32),
            pltpu.VMEM((16, 1024), BF),
            pltpu.VMEM((FRAME, 128), jnp.int32),
            pltpu.VMEM((BOX, 1024), F32),
            pltpu.VMEM((FUN, 128), jnp.int32),
            pltpu.VMEM((64, FRAME), jnp.int32),
            pltpu.VMEM((32, FRAME), jnp.int32),
            pltpu.VMEM((1024, 1024), BF),
            pltpu.VMEM((7, 16, 1024), BF),
            pltpu.VMEM((128, 1024), F32),
            pltpu.VMEM((FUN, 4, 8, 1024), F32),
            pltpu.VMEM((FUN, 4, 8, 1024), BF),
            pltpu.VMEM((384, 1024), F32),
            dma((3, 4)), dma((4, 4)), dma((10,)), dma((10,)), dma((7,)), dma((7,)),
            dma((9,)), dma((12,)), dma((11,)), dma((12,)), dma((4,)), dma((4,)),
            dma((12, 3)), dma((4, 3, 3)), dma((3,)),
        ],
        compiler_params=pltpu.CompilerParams(collective_id=0, has_side_effects=True),
        name="exchange",
    )(coeffs.reshape(FUN, 4, 8, 1024), kinetic, potential, centers.reshape(FUN, 128))
    filtered, gram_band = pl.pallas_call(
        write_kernel,
        out_shape=(
            jax.ShapeDtypeStruct((FUN, 4, 8, 1024), BF),
            jax.ShapeDtypeStruct((FUN, FRAME), F32),
        ),
        in_specs=[vmem, vmem],
        out_specs=(hbm, hbm),
        scratch_shapes=[dma((2,))],
        name="write",
    )(*[pltpu.with_memory_space_constraint(r, pltpu.VMEM) for r in results])
    return filtered.reshape(FUN, SUP, 1024), gram_band


def solution(mesh):
    placed = (P(("func", "box"), None, None), P(), P(), P(("func", "box"), None))
    return jax.shard_map(
        on_device,
        mesh=mesh,
        in_specs=placed,
        out_specs=(P(("func", "box"), None, None), P(("func", "box"), None)),
        check_vma=False,
    )
```

```python
import jax
import jax.numpy as jnp
from jax import lax
from jax.experimental import pallas as pl
from jax.experimental.pallas import tpu as pltpu
from jax.sharding import PartitionSpec as P

MESH = pl.DeviceIdType.MESH
BF = jnp.bfloat16
F32 = jnp.float32

SUP = 32
FUN = 24
BOX = 12
RING = 4
OWN = FUN * RING
FRAME = 256
LEFT = 80
SLICE = 256
BOX_ALL = 1536
FUN_ALL = 3072
W_HALO = 4
W_OWN = 6
LIVE = slice(16, 240)
VOLUME = 1.0 / (32 * 1024)

HALO = (
    (80, 0, 2, 176, -1),
    (144, 2, 2, 48, 1),
    (112, 0, 1, 208, -1),
    (112, 3, 1, 16, 1),
)
FORWARD = (
    (0, 0, 0, 24, -1),
    (3, 3, 0, 24, 1),
    (1, 0, 0, 24, -1),
    (2, 3, 0, 24, 1),
    (0, 1, 0, 24, -1),
    (3, 2, 0, 24, 1),
    (2, 0, 0, 16, -1),
    (1, 3, 8, 16, 1),
    (1, 1, 0, 8, -1),
    (2, 2, 16, 8, 1),
)


def exchange_kernel(
    coeffs, kinetic, pot_hbm, lanes_hbm, y_res, gram_out,
    frame, slots, gram_out_rows, back_a, back_b, back_c, back_d, gram, terms, sums, rows_out, rows_in, mixing, potb, boxes,
    pot, lanes_in, meta, starts, kin, v_win, pot_rows, pot_own, y_in, x_in,
    y_send, y_recv, x_send, x_recv, v_send, v_recv, s_send, s_recv, c_send, c_recv, bx_send, bx_recv,
    by_send, by_recv, kin_sem,
):
    me = lax.axis_index("func") * 16 + lax.axis_index("box")
    y = lax.rem(me, RING)
    base = me - y

    def dev(linear):
        wrapped = lax.rem(linear + 128, 128)
        return (lax.div(wrapped, 16), lax.rem(wrapped, 16))

    barrier = pltpu.get_barrier_semaphore()
    partners = [base + lax.rem(y + k, RING) for k in range(1, RING)] + [me + RING, me - RING]
    for partner in partners:
        pl.semaphore_signal(barrier, inc=1, device_id=dev(partner), device_id_type=MESH)

    loads = [
        pltpu.make_async_copy(src, dst, kin_sem.at[n])
        for n, (src, dst) in enumerate(((lanes_hbm, lanes_in), (pot_hbm, pot), (kinetic, kin)))
    ]
    for copy in loads:
        copy.start()

    pl.semaphore_wait(barrier, len(partners))

    started = []

    my_rows = pl.ds(pl.multiple_of(LEFT + FUN * y, 8), FUN)
    high = lax.div(y, 2)
    inner = lax.rem(lax.div(y + 1, 2), 2)

    for p in range(4):
        q0 = p + inner * ((0, 3, 1, 2)[p] - p)
        q = q0 + high * (3 - 2 * q0)
        for k in (2, 1, 3):
            yp = lax.rem(y + k, RING)
            copy = pltpu.make_async_remote_copy(
                src_ref=coeffs.at[:, q, :, pl.ds(pl.multiple_of(yp * SLICE, SLICE), SLICE)],
                dst_ref=frame.at[my_rows, q],
                send_sem=y_send.at[k - 1, p],
                recv_sem=y_recv.at[y, q],
                device_id=dev(base + yp),
                device_id_type=MESH,
            )
            copy.start()
            started.append(copy)
        pltpu.make_async_copy(
            coeffs.at[:, q, :, pl.ds(pl.multiple_of(y * SLICE, SLICE), SLICE)],
            frame.at[my_rows, q],
            y_recv.at[y, q],
        ).start()

    frame[16:48, 0:3] = jnp.zeros((32, 3, 8, SLICE), BF)
    frame[48:80, 0:2] = jnp.zeros((32, 2, 8, SLICE), BF)
    frame[176:208, 2:4] = jnp.zeros((32, 2, 8, SLICE), BF)
    frame[208:240, 1:4] = jnp.zeros((32, 3, 8, SLICE), BF)
    slots[:, 0:16, :] = jnp.zeros((SUP, 16, SLICE), BF)
    slots[:, 240:256, :] = jnp.zeros((SUP, 16, SLICE), BF)

    loads[0].wait()
    ring = lax.div(me, RING)
    flat = ring * OWN - LEFT + FUN_ALL
    top_line = lax.div(flat, 128)
    lines = [lanes_in[pl.ds(lax.rem(top_line + k, FUN_ALL // 128), 1), :] for k in range(3)]
    near = pltpu.roll(jnp.concatenate(lines, axis=1), 384 - lax.rem(flat, 128), 1)[:, 0:FRAME]
    row_lane = lax.broadcasted_iota(jnp.int32, (1, FRAME), 1)

    def pick(row, lane_at):
        return jnp.sum(jnp.where(row_lane == lane_at, row, 0), axis=1, keepdims=True)

    rel_row = near - pick(near, LEFT) + OWN
    rel_row = jnp.where(rel_row < 0, rel_row + BOX_ALL, rel_row)
    rel_row = jnp.where(rel_row >= BOX_ALL, rel_row - BOX_ALL, rel_row)
    low_row = OWN + 16
    top_row = pick(rel_row, LEFT + OWN - 1) + 16
    row_id = lax.broadcasted_iota(jnp.int32, (FRAME, FRAME), 0)
    col_id = lax.broadcasted_iota(jnp.int32, (FRAME, FRAME), 1)
    rel_tile = jnp.broadcast_to(rel_row, (FRAME, FRAME))
    rel_col = jnp.sum(
        jnp.where(row_id == col_id, rel_tile.astype(F32), 0.0), axis=1, keepdims=True
    ).astype(jnp.int32)
    boxes[...] = jnp.broadcast_to(rel_col, (FRAME, 128))
    sub_o = lax.broadcasted_iota(jnp.int32, (32, FRAME), 0)
    lane_o = lax.broadcasted_iota(jnp.int32, (32, FRAME), 1)
    rest_row = jnp.bitwise_and(rel_row, SUP - 1)
    spread = jnp.where(
        lax.shift_right_logical(lane_o, 3) == sub_o, jnp.broadcast_to(rest_row, (32, FRAME)), 0
    ).astype(F32).astype(BF)
    in_octet = jnp.bitwise_and(row_id, 7)
    by_fun = (in_octet == lax.shift_right_logical(col_id, 5)).astype(F32).astype(BF)
    by_low = (in_octet == jnp.bitwise_and(col_id, 7)).astype(F32).astype(BF)
    rest_fun = jnp.dot(spread, by_fun, preferred_element_type=F32).astype(jnp.int32)
    rest_low = jnp.dot(spread, by_low, preferred_element_type=F32).astype(jnp.int32)
    meta[0:32, :] = jnp.bitwise_and(rest_fun + lane_o, SUP - 1) * 8 + lax.shift_right_logical(lane_o, 5)
    meta[32:64, :] = jnp.bitwise_and(lane_o, 7) * SUP + jnp.bitwise_and(
        lax.shift_right_logical(lane_o, 3) - rest_low, SUP - 1
    )

    start_row = near - BOX * (me - 2)
    start_row = jnp.where(start_row < 0, start_row + BOX_ALL, start_row)
    start_row = jnp.where(start_row >= BOX_ALL, start_row - BOX_ALL, start_row)
    start_row = jnp.minimum(start_row, 127)
    spread = jnp.where(
        lax.shift_right_logical(lane_o, 3) == sub_o, jnp.broadcast_to(start_row, (32, FRAME)), 0
    ).astype(F32).astype(BF)
    starts[...] = jnp.dot(spread, by_fun, preferred_element_type=F32).astype(jnp.int32) + jnp.bitwise_and(
        lane_o, SUP - 1
    )

    arrived = set()

    def wait_piece(ys, q):
        if (ys, q) in arrived:
            return
        arrived.add((ys, q))
        piece = frame.at[pl.ds(LEFT + FUN * ys, FUN), q]
        pltpu.make_async_copy(piece, piece, y_recv.at[ys, q]).wait()

    forwards = []
    for n, (ys, q, first, count, to) in enumerate(FORWARD):
        wait_piece(ys, q)
        src = LEFT + FUN * ys + first
        copy = pltpu.make_async_remote_copy(
            src_ref=frame.at[pl.ds(src, count), q],
            dst_ref=frame.at[pl.ds(src - OWN * to, count), q],
            send_sem=x_send.at[n],
            recv_sem=x_recv.at[n],
            device_id=dev(me + RING * to),
            device_id_type=MESH,
        )
        copy.start()
        forwards.append(copy)

    def pairs(step_of, first, count, width):
        def several(step, carry):
            for k in range(width):
                step_of(first + width * step + k, carry)
            return carry

        lax.fori_loop(0, count // width, several, 0)

    def into_slots(pair, carry):
        parts = []
        for half in range(2):
            octet = 2 * pair + half
            select = (row_id == meta[pl.ds(octet, 1), :]).astype(F32).astype(BF)
            raw = frame[pl.ds(pl.multiple_of(8 * octet, 8), 8)]
            raw = raw.astype(F32).reshape(FRAME, SLICE).astype(BF)
            out = jnp.dot(select, raw, preferred_element_type=F32)
            parts.append(out.reshape(SUP, 8, SLICE))
        both = jnp.concatenate(parts, axis=1).astype(BF)
        slots[:, pl.ds(pl.multiple_of(16 * pair, 16), 16), :] = both
        return carry

    for copy in forwards:
        copy.wait_recv()
    pairs(into_slots, 1, 4, W_HALO)
    pairs(into_slots, 11, 4, W_HALO)
    for ys in range(RING):
        for q in range(4):
            wait_piece(ys, q)

    pairs(into_slots, 5, 6, W_OWN)

    def same_box(slot):
        box_row = rel_row + jnp.bitwise_and(slot - rel_row, SUP - 1)
        owned = jnp.logical_and(box_row >= low_row, box_row <= top_row)
        box_row = jnp.where(owned, box_row, -1)
        col = boxes[LIVE, :]
        box_col = col + jnp.bitwise_and(slot - col, SUP - 1)
        return box_col == box_row[:, 0:128], box_col == box_row[:, 128:256]

    gram[...] = jnp.zeros((FRAME, FRAME), F32)

    def gram_step(step, carry):
        lo, hi = gram[LIVE, 0:128], gram[LIVE, 128:256]
        for part in range(4):
            slot = 4 * step + part
            held = slots[slot]
            prod = lax.dot_general(held[LIVE], held, (((1,), (1,)), ((), ())), preferred_element_type=F32)
            same_lo, same_hi = same_box(slot)
            lo = lo + jnp.where(same_lo, prod[:, 0:128], 0.0)
            hi = hi + jnp.where(same_hi, prod[:, 128:256], 0.0)
        gram[LIVE, 0:128] = lo
        gram[LIVE, 128:256] = hi
        return carry

    lax.fori_loop(0, SUP // 4, gram_step, 0)
    scaled = gram[...] * VOLUME
    gram[...] = scaled
    high_part = scaled.astype(BF)
    rest = scaled - high_part.astype(F32)
    rest = jnp.sum(jnp.where(row_id == col_id, rest, 0.0), axis=1, keepdims=True)
    travels = jnp.where(col_id == FRAME - 1, rest, scaled)
    gram_out_rows[...] = travels.reshape(FRAME // 8, 8, FRAME).astype(BF)

    s_copies = []

    def send_terms(n, start, slot, target):
        copy = pltpu.make_async_remote_copy(
            src_ref=gram_out_rows.at[pl.ds(start, FUN // 8)],
            dst_ref=terms.at[slot],
            send_sem=s_send.at[n],
            recv_sem=s_recv.at[slot],
            device_id=dev(target),
            device_id_type=MESH,
        )
        copy.start()
        s_copies.append(copy)

    for yp in range(1, 4):
        send_terms(2 + yp, 3 * yp - 2, 8 + y, base - RING + yp)
    for yp in range(0, 3):
        send_terms(6 + yp, 22 + 3 * yp, y, base + RING + yp)
    for k in range(1, 4):
        yp = lax.rem(y + k, RING)
        send_terms(k - 1, LEFT // 8 + 3 * yp, 4 + y, base + yp)

    def wait_terms(slot):
        pltpu.make_async_copy(terms.at[slot], terms.at[slot], s_recv.at[slot]).wait()

    def arrived_terms(slot):
        return terms[slot].astype(F32).reshape(FUN, FRAME)

    sums[0] = jnp.zeros((FUN, FRAME), F32)
    sums[2] = jnp.zeros((FUN, FRAME), F32)
    sums[1] = gram[my_rows, :]
    for k in range(1, 4):
        slot = 4 + lax.rem(y + k, RING)
        wait_terms(slot)
        sums[1] += arrived_terms(slot)

    @pl.when(y <= 2)
    def _():
        for ys in range(RING):
            wait_terms(ys)
        sums[0] = arrived_terms(0) + arrived_terms(1) + arrived_terms(2) + arrived_terms(3)

    @pl.when(y >= 1)
    def _():
        for ys in range(RING):
            wait_terms(8 + ys)
        sums[2] = arrived_terms(8) + arrived_terms(9) + arrived_terms(10) + arrived_terms(11)

    short_lane = lax.broadcasted_iota(jnp.int32, (FUN, FRAME), 1)
    short_sub = lax.broadcasted_iota(jnp.int32, (FUN, FRAME), 0)
    for n, at in enumerate((176, LEFT, -16)):
        held = sums[n]
        low_part = held[:, FRAME - 1 : FRAME]
        held = held + jnp.where(short_lane == short_sub + (FUN * y + at), low_part, 0.0)
        sums[n] = jnp.where(short_lane == FRAME - 1, 0.0, held)

    pad = jnp.zeros((FUN, FRAME), F32)
    wide = jnp.concatenate([sums[0], pad], axis=1)
    wide += pltpu.roll(jnp.concatenate([sums[1], pad], axis=1), 96, 1)
    wide += pltpu.roll(jnp.concatenate([sums[2], pad], axis=1), 192, 1)
    lane = lax.broadcasted_iota(jnp.int32, (FUN, 512), 1)
    sub = lax.broadcasted_iota(jnp.int32, (FUN, 512), 0)
    fixed = (1.5 * (lane == sub + (FUN * y + 176)).astype(F32) - 0.5 * wide)
    rows_out[0] = fixed[:, 0:256].astype(BF)
    rows_out[1] = pltpu.roll(fixed, 512 - 96, 1)[:, 0:256].astype(BF)
    rows_out[2] = pltpu.roll(fixed, 512 - 192, 1)[:, 0:256].astype(BF)

    c_copies = []

    def send_rows(n, which, slot, target):
        copy = pltpu.make_async_remote_copy(
            src_ref=rows_out.at[which],
            dst_ref=rows_in.at[slot],
            send_sem=c_send.at[n],
            recv_sem=c_recv.at[slot],
            device_id=dev(target),
            device_id_type=MESH,
        )
        copy.start()
        return copy

    @pl.when(y <= 2)
    def _():
        for yp in range(RING):
            send_rows(3 + yp, 0, 8 + y, base - RING + yp)

    @pl.when(y >= 1)
    def _():
        for yp in range(RING):
            send_rows(7 + yp, 2, y, base + RING + yp)

    own_rows = [
        send_rows(k - 1, 1, 4 + y, base + lax.rem(y + k, RING)) for k in range(1, 4)
    ]

    band = pltpu.roll(wide, 512 - 49 - FUN * y, 1)
    for bit in range(5):
        moved = pltpu.roll(band, 512 - (1 << bit), 1)
        band = jnp.where(jnp.bitwise_and(sub, 1 << bit) != 0, moved, band)
    gram_out[...] = jnp.where(lane[:, 0:256] == 255, 0.0, band[:, 0:256])

    def wait_rows(slot):
        pltpu.make_async_copy(rows_in.at[slot], rows_in.at[slot], c_recv.at[slot]).wait()

    mixing[0:16, :] = jnp.zeros((16, FRAME), F32)
    mixing[240:256, :] = jnp.zeros((16, FRAME), F32)
    mixing[my_rows, :] = rows_out[1].astype(F32)
    for k in range(1, 4):
        ys = lax.rem(y + k, RING)
        wait_rows(4 + ys)
        mixing[pl.ds(pl.multiple_of(LEFT + FUN * ys, 8), FUN), :] = rows_in[4 + ys].astype(F32)
    for ys in range(0, 3):
        wait_rows(8 + ys)
        mixing[176 + FUN * ys : 200 + FUN * ys, :] = rows_in[8 + ys].astype(F32)
    for ys in range(1, 4):
        wait_rows(ys)
        mixing[FUN * ys - 16 : FUN * ys + 8, :] = rows_in[ys].astype(F32)

    loads[1].wait()
    potb[0:BOX, :] = pot[...].astype(BF)
    potb[BOX:16, :] = jnp.zeros((16 - BOX, 1024), BF)
    v_copies = []
    for o in range(-2, 5):
        if o == 0:
            copy = pltpu.make_async_copy(potb, v_win.at[2], v_recv.at[2])
        else:
            copy = pltpu.make_async_remote_copy(
                src_ref=potb,
                dst_ref=v_win.at[o + 2],
                send_sem=v_send.at[o + 2],
                recv_sem=v_recv.at[o + 2],
                device_id=dev(me - o),
                device_id_type=MESH,
            )
        copy.start()
        v_copies.append(copy)

    def mix_step(step, carry):
        for part in range(4):
            slot = 4 * step + part
            same_lo, same_hi = same_box(slot)
            mix = jnp.concatenate(
                [jnp.where(same_lo, mixing[LIVE, 0:128], 0.0), jnp.where(same_hi, mixing[LIVE, 128:256], 0.0)], axis=1
            ).astype(BF)
            slots[slot, LIVE, :] = jnp.dot(mix, slots[slot], preferred_element_type=F32).astype(BF)
        return carry

    lax.fori_loop(0, SUP // 4, mix_step, 0)

    for copy in forwards:
        copy.wait_send()

    def out_of_slots(pair, carry):
        both = slots[:, pl.ds(pl.multiple_of(16 * pair, 16), 16), :].astype(F32)
        for half in range(2):
            octet = 2 * pair + half
            select = (row_id == meta[pl.ds(32 + octet, 1), :]).astype(F32).astype(BF)
            part = both[:, 8 * half : 8 * half + 8, :].reshape(FRAME, SLICE).astype(BF)
            out = jnp.dot(select, part, preferred_element_type=F32)
            frame[pl.ds(pl.multiple_of(8 * octet, 8), 8)] = out.reshape(8, 4, 8, SLICE).astype(BF)
        return carry

    backs = (back_a, back_b, back_c, back_d)
    x_backs = []
    lanes = pl.ds(pl.multiple_of(y * SLICE, SLICE), SLICE)

    def halo_back(n):
        src, q, nq, dst, to = HALO[n]
        pairs(out_of_slots, dst // 16, 2, 2)
        copy = pltpu.make_async_remote_copy(
            src_ref=frame.at[pl.ds(dst, 32), pl.ds(q, nq)],
            dst_ref=backs[n],
            send_sem=bx_send.at[n],
            recv_sem=bx_recv.at[n],
            device_id=dev(me - RING * to),
            device_id_type=MESH,
        )
        copy.start()
        x_backs.append(copy)

    def merge(n):
        src, q, nq, dst, to = HALO[n]
        x_backs[n].wait_recv()
        mine = frame[src : src + 32, q : q + nq].astype(F32)
        frame[src : src + 32, q : q + nq] = (mine + backs[n][...].astype(F32)).astype(BF)

    def quarters(octet):
        unit = octet // 4 if isinstance(octet, int) else lax.div(octet, 4)
        half = (unit + 1) // 3 if isinstance(octet, int) else lax.div(unit + 1, 3)
        late = (unit + 2) // 3 if isinstance(octet, int) else lax.div(unit + 2, 3)
        return ((2 - unit, 2),), ((2 * half, 1), (1 + 2 * late, 1))

    def home_part(octet, n, which):
        q, nq = quarters(octet)[which][n]
        return frame.at[pl.ds(LEFT + 8 * octet, 8), pl.ds(q, nq)]

    def send_home(octets, which):
        for octet in octets:
            yp, j = octet // 3, octet % 3
            for n, (q, nq) in enumerate(quarters(octet)[which]):
                src = home_part(octet, n, which)
                dst = y_in.at[pl.ds(8 * j, 8), pl.ds(q, nq), :, lanes]
                kind = which + n

                @pl.when(y != yp)
                def _():
                    pltpu.make_async_remote_copy(
                        src_ref=src,
                        dst_ref=dst,
                        send_sem=by_send.at[octet, kind],
                        recv_sem=by_recv.at[y, j, kind],
                        device_id=dev(base + yp),
                        device_id_type=MESH,
                    ).start()

                @pl.when(y == yp)
                def _():
                    pltpu.make_async_copy(src, dst, by_recv.at[y, j, kind]).start()

    halo_back(0)
    halo_back(1)
    pairs(out_of_slots, 5, 3, 3)
    send_home(range(0, 6), 0)
    halo_back(2)
    halo_back(3)
    pairs(out_of_slots, 8, 3, 3)
    send_home(range(6, 12), 0)
    merge(0)
    send_home(range(0, 4), 1)
    merge(1)
    send_home(range(8, 12), 1)
    merge(2)
    merge(3)
    send_home(range(4, 8), 1)

    for copy in v_copies:
        if copy is v_copies[2]:
            copy.wait()
        else:
            copy.wait_recv()
    for k in range(7):
        pot_rows[BOX * k : BOX * k + BOX, :] = v_win[k].astype(F32)[0:BOX]
    pot_rows[7 * BOX : 128, :] = jnp.zeros((128 - 7 * BOX, 1024), F32)

    near_rows = pot_rows[...].astype(BF)
    row_of = lax.broadcasted_iota(jnp.int32, (128, FRAME), 0)
    for j in range(3):
        select = (row_of == starts[pl.ds(LEFT // 8 + 3 * y + j, 1), :]).astype(F32).astype(BF)
        local = lax.dot_general(select, near_rows, (((0,), (0,)), ((), ())), preferred_element_type=F32)
        pot_own[8 * j : 8 * j + 8] = local.reshape(8, 4, 8, 1024)

    loads[2].wait()
    for which in range(2):
        for k in (0, 1, 3, 2):
            ys = lax.rem(y + k, RING)
            cols = pl.ds(pl.multiple_of(ys * SLICE, SLICE), SLICE)
            for j in range(3):
                for n, (q, nq) in enumerate(quarters(3 * y + j)[which]):
                    part = y_in.at[pl.ds(8 * j, 8), pl.ds(q, nq), :, cols]
                    pltpu.make_async_copy(part, part, by_recv.at[ys, j, which + n]).wait()
            held, local = [], []
            for j in range(3):
                for n, (q, nq) in enumerate(quarters(3 * y + j)[which]):
                    part = (slice(8 * j, 8 * j + 8), pl.ds(q, nq), slice(None), cols)
                    held.append(y_in[part].astype(F32).reshape(64 * nq, SLICE))
                    local.append(pot_own[part].reshape(64 * nq, SLICE))
            held = jnp.concatenate(held, axis=0)
            local = jnp.concatenate(local, axis=0)
            applied = jnp.dot(held.astype(BF), kin[cols, :], preferred_element_type=F32)
            if k == 0:
                x_in[...] = applied
            else:
                x_in[...] += applied
            x_in[:, cols] += local * held
        at = 0
        for j in range(3):
            for n, (q, nq) in enumerate(quarters(3 * y + j)[which]):
                piece = x_in[at : at + 64 * nq, :].astype(BF).astype(F32)
                y_res[8 * j : 8 * j + 8, pl.ds(q, nq)] = piece.reshape(8, nq, 8, 1024).astype(BF)
                at += 64 * nq

    for copy in started:
        copy.wait_send()
    for k, copy in enumerate(v_copies):
        if k != 2:
            copy.wait_send()
    for copy in s_copies:
        copy.wait_send()
    for copy in own_rows:
        copy.wait_send()

    @pl.when(y <= 2)
    def _():
        for yp in range(RING):
            pltpu.make_async_copy(rows_out.at[0], rows_out.at[0], c_send.at[3 + yp]).wait()

    @pl.when(y >= 1)
    def _():
        for yp in range(RING):
            pltpu.make_async_copy(rows_out.at[2], rows_out.at[2], c_send.at[7 + yp]).wait()

    for copy in x_backs:
        copy.wait_send()
    for octet in range(12):
        for which in range(2):
            for n in range(which + 1):
                part = home_part(octet, n, which)

                @pl.when(y != octet // 3)
                def _():
                    pltpu.make_async_copy(part, part, by_send.at[octet, which + n]).wait()


def write_kernel(pieces, rows, pieces_out, rows_out, sem):
    copies = [
        pltpu.make_async_copy(pieces, pieces_out, sem.at[0]),
        pltpu.make_async_copy(rows, rows_out, sem.at[1]),
    ]
    for copy in copies:
        copy.start()
    for copy in copies:
        copy.wait()


def on_device(coeffs, centers, kinetic, potential):
    hbm = pl.BlockSpec(memory_space=pl.ANY)
    vmem = pl.BlockSpec(memory_space=pltpu.VMEM)
    dma = pltpu.SemaphoreType.DMA
    results = pl.pallas_call(
        exchange_kernel,
        out_shape=(
            pltpu.VMEM((FUN, 4, 8, 1024), BF),
            pltpu.VMEM((FUN, FRAME), F32),
        ),
        in_specs=[hbm, hbm, hbm, hbm],
        out_specs=(vmem, vmem),
        scratch_shapes=[
            pltpu.VMEM((FRAME, 4, 8, SLICE), BF),
            pltpu.VMEM((SUP, FRAME, SLICE), BF),
            pltpu.VMEM((FRAME // 8, 8, FRAME), BF),
            pltpu.VMEM((32, 2, 8, SLICE), BF),
            pltpu.VMEM((32, 2, 8, SLICE), BF),
            pltpu.VMEM((32, 1, 8, SLICE), BF),
            pltpu.VMEM((32, 1, 8, SLICE), BF),
            pltpu.VMEM((FRAME, FRAME), F32),
            pltpu.VMEM((12, FUN // 8, 8, FRAME), BF),
            pltpu.VMEM((3, FUN, FRAME), F32),
            pltpu.VMEM((3, FUN, FRAME), BF),
            pltpu.VMEM((12, FUN, FRAME), BF),
            pltpu.VMEM((FRAME, FRAME), F32),
            pltpu.VMEM((16, 1024), BF),
            pltpu.VMEM((FRAME, 128), jnp.int32),
            pltpu.VMEM((BOX, 1024), F32),
            pltpu.VMEM((FUN, 128), jnp.int32),
            pltpu.VMEM((64, FRAME), jnp.int32),
            pltpu.VMEM((32, FRAME), jnp.int32),
            pltpu.VMEM((1024, 1024), BF),
            pltpu.VMEM((7, 16, 1024), BF),
            pltpu.VMEM((128, 1024), F32),
            pltpu.VMEM((FUN, 4, 8, 1024), F32),
            pltpu.VMEM((FUN, 4, 8, 1024), BF),
            pltpu.VMEM((384, 1024), F32),
            dma((3, 4)), dma((4, 4)), dma((10,)), dma((10,)), dma((7,)), dma((7,)),
            dma((9,)), dma((12,)), dma((11,)), dma((12,)), dma((4,)), dma((4,)),
            dma((12, 3)), dma((4, 3, 3)), dma((3,)),
        ],
        compiler_params=pltpu.CompilerParams(collective_id=0, has_side_effects=True),
        name="exchange",
    )(coeffs.reshape(FUN, 4, 8, 1024), kinetic, potential, centers.reshape(FUN, 128))
    filtered, gram_band = pl.pallas_call(
        write_kernel,
        out_shape=(
            jax.ShapeDtypeStruct((FUN, 4, 8, 1024), BF),
            jax.ShapeDtypeStruct((FUN, FRAME), F32),
        ),
        in_specs=[vmem, vmem],
        out_specs=(hbm, hbm),
        scratch_shapes=[dma((2,))],
        name="write",
    )(*[pltpu.with_memory_space_constraint(r, pltpu.VMEM) for r in results])
    return filtered.reshape(FUN, SUP, 1024), gram_band


def solution(mesh):
    placed = (P(("func", "box"), None, None), P(), P(), P(("func", "box"), None))
    return jax.shard_map(
        on_device,
        mesh=mesh,
        in_specs=placed,
        out_specs=(P(("func", "box"), None, None), P(("func", "box"), None)),
        check_vma=False,
    )
```

```python
import jax
import jax.numpy as jnp
from jax import lax
from jax.experimental import pallas as pl
from jax.experimental.pallas import tpu as pltpu
from jax.sharding import PartitionSpec as P

MESH = pl.DeviceIdType.MESH
BF = jnp.bfloat16
F32 = jnp.float32

SUP = 32
FUN = 24
BOX = 12
RING = 4
OWN = FUN * RING
FRAME = 256
LEFT = 80
SLICE = 256
BOX_ALL = 1536
FUN_ALL = 3072
W_HALO = 4
W_OWN = 6
LIVE = slice(16, 240)
VOLUME = 1.0 / (32 * 1024)

HALO = (
    (80, 0, 2, 176, -1),
    (144, 2, 2, 48, 1),
    (112, 0, 1, 208, -1),
    (112, 3, 1, 16, 1),
)
FORWARD = (
    (0, 0, 0, 24, -1),
    (3, 3, 0, 24, 1),
    (1, 0, 0, 24, -1),
    (2, 3, 0, 24, 1),
    (0, 1, 0, 24, -1),
    (3, 2, 0, 24, 1),
    (2, 0, 0, 16, -1),
    (1, 3, 8, 16, 1),
    (1, 1, 0, 8, -1),
    (2, 2, 16, 8, 1),
)


def exchange_kernel(
    coeffs, kinetic, pot_hbm, lanes_hbm, y_res, gram_out,
    frame, slots, gram_out_rows, back_a, back_b, back_c, back_d, gram, terms, sums, rows_out, rows_in, mixing, potb, boxes,
    pot, lanes_in, meta, starts, kin, v_win, pot_rows, pot_own, y_in, x_in,
    y_send, y_recv, x_send, x_recv, v_send, v_recv, s_send, s_recv, c_send, c_recv, bx_send, bx_recv,
    by_send, by_recv, kin_sem,
):
    me = lax.axis_index("func") * 16 + lax.axis_index("box")
    y = lax.rem(me, RING)
    base = me - y

    def dev(linear):
        wrapped = lax.rem(linear + 128, 128)
        return (lax.div(wrapped, 16), lax.rem(wrapped, 16))

    barrier = pltpu.get_barrier_semaphore()
    partners = [base + lax.rem(y + k, RING) for k in range(1, RING)] + [me + RING, me - RING]
    for partner in partners:
        pl.semaphore_signal(barrier, inc=1, device_id=dev(partner), device_id_type=MESH)

    loads = [
        pltpu.make_async_copy(src, dst, kin_sem.at[n])
        for n, (src, dst) in enumerate(((lanes_hbm, lanes_in), (pot_hbm, pot), (kinetic, kin)))
    ]
    for copy in loads:
        copy.start()

    pl.semaphore_wait(barrier, len(partners))

    started = []

    my_rows = pl.ds(pl.multiple_of(LEFT + FUN * y, 8), FUN)
    high = lax.div(y, 2)
    inner = lax.rem(lax.div(y + 1, 2), 2)

    for p in range(4):
        q0 = p + inner * ((0, 3, 1, 2)[p] - p)
        q = q0 + high * (3 - 2 * q0)
        for k in (2, 1, 3):
            yp = lax.rem(y + k, RING)
            copy = pltpu.make_async_remote_copy(
                src_ref=coeffs.at[:, q, :, pl.ds(pl.multiple_of(yp * SLICE, SLICE), SLICE)],
                dst_ref=frame.at[my_rows, q],
                send_sem=y_send.at[k - 1, p],
                recv_sem=y_recv.at[y, q],
                device_id=dev(base + yp),
                device_id_type=MESH,
            )
            copy.start()
            started.append(copy)
        pltpu.make_async_copy(
            coeffs.at[:, q, :, pl.ds(pl.multiple_of(y * SLICE, SLICE), SLICE)],
            frame.at[my_rows, q],
            y_recv.at[y, q],
        ).start()

    frame[16:48, 0:3] = jnp.zeros((32, 3, 8, SLICE), BF)
    frame[48:80, 0:2] = jnp.zeros((32, 2, 8, SLICE), BF)
    frame[176:208, 2:4] = jnp.zeros((32, 2, 8, SLICE), BF)
    frame[208:240, 1:4] = jnp.zeros((32, 3, 8, SLICE), BF)
    slots[:, 0:16, :] = jnp.zeros((SUP, 16, SLICE), BF)
    slots[:, 240:256, :] = jnp.zeros((SUP, 16, SLICE), BF)

    loads[0].wait()
    ring = lax.div(me, RING)
    flat = ring * OWN - LEFT + FUN_ALL
    top_line = lax.div(flat, 128)
    lines = [lanes_in[pl.ds(lax.rem(top_line + k, FUN_ALL // 128), 1), :] for k in range(3)]
    near = pltpu.roll(jnp.concatenate(lines, axis=1), 384 - lax.rem(flat, 128), 1)[:, 0:FRAME]
    row_lane = lax.broadcasted_iota(jnp.int32, (1, FRAME), 1)

    def pick(row, lane_at):
        return jnp.sum(jnp.where(row_lane == lane_at, row, 0), axis=1, keepdims=True)

    rel_row = near - pick(near, LEFT) + OWN
    rel_row = jnp.where(rel_row < 0, rel_row + BOX_ALL, rel_row)
    rel_row = jnp.where(rel_row >= BOX_ALL, rel_row - BOX_ALL, rel_row)
    low_row = OWN + 16
    top_row = pick(rel_row, LEFT + OWN - 1) + 16
    row_id = lax.broadcasted_iota(jnp.int32, (FRAME, FRAME), 0)
    col_id = lax.broadcasted_iota(jnp.int32, (FRAME, FRAME), 1)
    rel_tile = jnp.broadcast_to(rel_row, (FRAME, FRAME))
    rel_col = jnp.sum(
        jnp.where(row_id == col_id, rel_tile.astype(F32), 0.0), axis=1, keepdims=True
    ).astype(jnp.int32)
    boxes[...] = jnp.broadcast_to(rel_col, (FRAME, 128))
    sub_o = lax.broadcasted_iota(jnp.int32, (32, FRAME), 0)
    lane_o = lax.broadcasted_iota(jnp.int32, (32, FRAME), 1)
    rest_row = jnp.bitwise_and(rel_row, SUP - 1)
    spread = jnp.where(
        lax.shift_right_logical(lane_o, 3) == sub_o, jnp.broadcast_to(rest_row, (32, FRAME)), 0
    ).astype(F32).astype(BF)
    in_octet = jnp.bitwise_and(row_id, 7)
    by_fun = (in_octet == lax.shift_right_logical(col_id, 5)).astype(F32).astype(BF)
    by_low = (in_octet == jnp.bitwise_and(col_id, 7)).astype(F32).astype(BF)
    rest_fun = jnp.dot(spread, by_fun, preferred_element_type=F32).astype(jnp.int32)
    rest_low = jnp.dot(spread, by_low, preferred_element_type=F32).astype(jnp.int32)
    meta[0:32, :] = jnp.bitwise_and(rest_fun + lane_o, SUP - 1) * 8 + lax.shift_right_logical(lane_o, 5)
    meta[32:64, :] = jnp.bitwise_and(lane_o, 7) * SUP + jnp.bitwise_and(
        lax.shift_right_logical(lane_o, 3) - rest_low, SUP - 1
    )

    start_row = near - BOX * (me - 2)
    start_row = jnp.where(start_row < 0, start_row + BOX_ALL, start_row)
    start_row = jnp.where(start_row >= BOX_ALL, start_row - BOX_ALL, start_row)
    start_row = jnp.minimum(start_row, 127)
    spread = jnp.where(
        lax.shift_right_logical(lane_o, 3) == sub_o, jnp.broadcast_to(start_row, (32, FRAME)), 0
    ).astype(F32).astype(BF)
    starts[...] = jnp.dot(spread, by_fun, preferred_element_type=F32).astype(jnp.int32) + jnp.bitwise_and(
        lane_o, SUP - 1
    )

    arrived = set()

    def wait_piece(ys, q):
        if (ys, q) in arrived:
            return
        arrived.add((ys, q))
        piece = frame.at[pl.ds(LEFT + FUN * ys, FUN), q]
        pltpu.make_async_copy(piece, piece, y_recv.at[ys, q]).wait()

    forwards = []
    for n, (ys, q, first, count, to) in enumerate(FORWARD):
        wait_piece(ys, q)
        src = LEFT + FUN * ys + first
        copy = pltpu.make_async_remote_copy(
            src_ref=frame.at[pl.ds(src, count), q],
            dst_ref=frame.at[pl.ds(src - OWN * to, count), q],
            send_sem=x_send.at[n],
            recv_sem=x_recv.at[n],
            device_id=dev(me + RING * to),
            device_id_type=MESH,
        )
        copy.start()
        forwards.append(copy)

    def pairs(step_of, first, count, width):
        def several(step, carry):
            for k in range(width):
                step_of(first + width * step + k, carry)
            return carry

        lax.fori_loop(0, count // width, several, 0)

    def into_slots(pair, carry):
        parts = []
        for half in range(2):
            octet = 2 * pair + half
            select = (row_id == meta[pl.ds(octet, 1), :]).astype(F32).astype(BF)
            raw = frame[pl.ds(pl.multiple_of(8 * octet, 8), 8)]
            raw = raw.astype(F32).reshape(FRAME, SLICE).astype(BF)
            out = jnp.dot(select, raw, preferred_element_type=F32)
            parts.append(out.reshape(SUP, 8, SLICE))
        both = jnp.concatenate(parts, axis=1).astype(BF)
        slots[:, pl.ds(pl.multiple_of(16 * pair, 16), 16), :] = both
        return carry

    for copy in forwards:
        copy.wait_recv()
    pairs(into_slots, 1, 4, W_HALO)
    pairs(into_slots, 11, 4, W_HALO)
    for ys in range(RING):
        for q in range(4):
            wait_piece(ys, q)

    pairs(into_slots, 5, 6, W_OWN)

    def same_box(slot):
        box_row = rel_row + jnp.bitwise_and(slot - rel_row, SUP - 1)
        owned = jnp.logical_and(box_row >= low_row, box_row <= top_row)
        box_row = jnp.where(owned, box_row, -1)
        col = boxes[LIVE, :]
        box_col = col + jnp.bitwise_and(slot - col, SUP - 1)
        return box_col == box_row[:, 0:128], box_col == box_row[:, 128:256]

    gram[...] = jnp.zeros((FRAME, FRAME), F32)

    def gram_step(step, carry):
        lo, hi = gram[LIVE, 0:128], gram[LIVE, 128:256]
        for part in range(8):
            slot = 8 * step + part
            held = slots[slot]
            prod = lax.dot_general(held[LIVE], held, (((1,), (1,)), ((), ())), preferred_element_type=F32)
            same_lo, same_hi = same_box(slot)
            lo = lo + jnp.where(same_lo, prod[:, 0:128], 0.0)
            hi = hi + jnp.where(same_hi, prod[:, 128:256], 0.0)
        gram[LIVE, 0:128] = lo
        gram[LIVE, 128:256] = hi
        return carry

    lax.fori_loop(0, SUP // 8, gram_step, 0)
    scaled = gram[...] * VOLUME
    gram[...] = scaled
    high_part = scaled.astype(BF)
    rest = scaled - high_part.astype(F32)
    rest = jnp.sum(jnp.where(row_id == col_id, rest, 0.0), axis=1, keepdims=True)
    travels = jnp.where(col_id == FRAME - 1, rest, scaled)
    gram_out_rows[...] = travels.reshape(FRAME // 8, 8, FRAME).astype(BF)

    s_copies = []

    def send_terms(n, start, slot, target):
        copy = pltpu.make_async_remote_copy(
            src_ref=gram_out_rows.at[pl.ds(start, FUN // 8)],
            dst_ref=terms.at[slot],
            send_sem=s_send.at[n],
            recv_sem=s_recv.at[slot],
            device_id=dev(target),
            device_id_type=MESH,
        )
        copy.start()
        s_copies.append(copy)

    for yp in range(1, 4):
        send_terms(2 + yp, 3 * yp - 2, 8 + y, base - RING + yp)
    for yp in range(0, 3):
        send_terms(6 + yp, 22 + 3 * yp, y, base + RING + yp)
    for k in range(1, 4):
        yp = lax.rem(y + k, RING)
        send_terms(k - 1, LEFT // 8 + 3 * yp, 4 + y, base + yp)

    def wait_terms(slot):
        pltpu.make_async_copy(terms.at[slot], terms.at[slot], s_recv.at[slot]).wait()

    def arrived_terms(slot):
        return terms[slot].astype(F32).reshape(FUN, FRAME)

    sums[0] = jnp.zeros((FUN, FRAME), F32)
    sums[2] = jnp.zeros((FUN, FRAME), F32)
    sums[1] = gram[my_rows, :]
    for k in range(1, 4):
        slot = 4 + lax.rem(y + k, RING)
        wait_terms(slot)
        sums[1] += arrived_terms(slot)

    @pl.when(y <= 2)
    def _():
        for ys in range(RING):
            wait_terms(ys)
        sums[0] = arrived_terms(0) + arrived_terms(1) + arrived_terms(2) + arrived_terms(3)

    @pl.when(y >= 1)
    def _():
        for ys in range(RING):
            wait_terms(8 + ys)
        sums[2] = arrived_terms(8) + arrived_terms(9) + arrived_terms(10) + arrived_terms(11)

    short_lane = lax.broadcasted_iota(jnp.int32, (FUN, FRAME), 1)
    short_sub = lax.broadcasted_iota(jnp.int32, (FUN, FRAME), 0)
    for n, at in enumerate((176, LEFT, -16)):
        held = sums[n]
        low_part = held[:, FRAME - 1 : FRAME]
        held = held + jnp.where(short_lane == short_sub + (FUN * y + at), low_part, 0.0)
        sums[n] = jnp.where(short_lane == FRAME - 1, 0.0, held)

    pad = jnp.zeros((FUN, FRAME), F32)
    wide = jnp.concatenate([sums[0], pad], axis=1)
    wide += pltpu.roll(jnp.concatenate([sums[1], pad], axis=1), 96, 1)
    wide += pltpu.roll(jnp.concatenate([sums[2], pad], axis=1), 192, 1)
    lane = lax.broadcasted_iota(jnp.int32, (FUN, 512), 1)
    sub = lax.broadcasted_iota(jnp.int32, (FUN, 512), 0)
    fixed = (1.5 * (lane == sub + (FUN * y + 176)).astype(F32) - 0.5 * wide)
    rows_out[0] = fixed[:, 0:256].astype(BF)
    rows_out[1] = pltpu.roll(fixed, 512 - 96, 1)[:, 0:256].astype(BF)
    rows_out[2] = pltpu.roll(fixed, 512 - 192, 1)[:, 0:256].astype(BF)

    c_copies = []

    def send_rows(n, which, slot, target):
        copy = pltpu.make_async_remote_copy(
            src_ref=rows_out.at[which],
            dst_ref=rows_in.at[slot],
            send_sem=c_send.at[n],
            recv_sem=c_recv.at[slot],
            device_id=dev(target),
            device_id_type=MESH,
        )
        copy.start()
        return copy

    @pl.when(y <= 2)
    def _():
        for yp in range(RING):
            send_rows(3 + yp, 0, 8 + y, base - RING + yp)

    @pl.when(y >= 1)
    def _():
        for yp in range(RING):
            send_rows(7 + yp, 2, y, base + RING + yp)

    own_rows = [
        send_rows(k - 1, 1, 4 + y, base + lax.rem(y + k, RING)) for k in range(1, 4)
    ]

    band = pltpu.roll(wide, 512 - 49 - FUN * y, 1)
    for bit in range(5):
        moved = pltpu.roll(band, 512 - (1 << bit), 1)
        band = jnp.where(jnp.bitwise_and(sub, 1 << bit) != 0, moved, band)
    gram_out[...] = jnp.where(lane[:, 0:256] == 255, 0.0, band[:, 0:256])

    def wait_rows(slot):
        pltpu.make_async_copy(rows_in.at[slot], rows_in.at[slot], c_recv.at[slot]).wait()

    mixing[0:16, :] = jnp.zeros((16, FRAME), F32)
    mixing[240:256, :] = jnp.zeros((16, FRAME), F32)
    mixing[my_rows, :] = rows_out[1].astype(F32)
    for k in range(1, 4):
        ys = lax.rem(y + k, RING)
        wait_rows(4 + ys)
        mixing[pl.ds(pl.multiple_of(LEFT + FUN * ys, 8), FUN), :] = rows_in[4 + ys].astype(F32)
    for ys in range(0, 3):
        wait_rows(8 + ys)
        mixing[176 + FUN * ys : 200 + FUN * ys, :] = rows_in[8 + ys].astype(F32)
    for ys in range(1, 4):
        wait_rows(ys)
        mixing[FUN * ys - 16 : FUN * ys + 8, :] = rows_in[ys].astype(F32)

    loads[1].wait()
    potb[0:BOX, :] = pot[...].astype(BF)
    potb[BOX:16, :] = jnp.zeros((16 - BOX, 1024), BF)
    v_copies = []
    for o in range(-2, 5):
        if o == 0:
            copy = pltpu.make_async_copy(potb, v_win.at[2], v_recv.at[2])
        else:
            copy = pltpu.make_async_remote_copy(
                src_ref=potb,
                dst_ref=v_win.at[o + 2],
                send_sem=v_send.at[o + 2],
                recv_sem=v_recv.at[o + 2],
                device_id=dev(me - o),
                device_id_type=MESH,
            )
        copy.start()
        v_copies.append(copy)

    def mix_step(step, carry):
        for part in range(8):
            slot = 8 * step + part
            same_lo, same_hi = same_box(slot)
            mix = jnp.concatenate(
                [jnp.where(same_lo, mixing[LIVE, 0:128], 0.0), jnp.where(same_hi, mixing[LIVE, 128:256], 0.0)], axis=1
            ).astype(BF)
            slots[slot, LIVE, :] = jnp.dot(mix, slots[slot], preferred_element_type=F32).astype(BF)
        return carry

    lax.fori_loop(0, SUP // 8, mix_step, 0)

    for copy in forwards:
        copy.wait_send()

    def out_of_slots(pair, carry):
        both = slots[:, pl.ds(pl.multiple_of(16 * pair, 16), 16), :].astype(F32)
        for half in range(2):
            octet = 2 * pair + half
            select = (row_id == meta[pl.ds(32 + octet, 1), :]).astype(F32).astype(BF)
            part = both[:, 8 * half : 8 * half + 8, :].reshape(FRAME, SLICE).astype(BF)
            out = jnp.dot(select, part, preferred_element_type=F32)
            frame[pl.ds(pl.multiple_of(8 * octet, 8), 8)] = out.reshape(8, 4, 8, SLICE).astype(BF)
        return carry

    backs = (back_a, back_b, back_c, back_d)
    x_backs = []
    lanes = pl.ds(pl.multiple_of(y * SLICE, SLICE), SLICE)

    def halo_back(n):
        src, q, nq, dst, to = HALO[n]
        pairs(out_of_slots, dst // 16, 2, 2)
        copy = pltpu.make_async_remote_copy(
            src_ref=frame.at[pl.ds(dst, 32), pl.ds(q, nq)],
            dst_ref=backs[n],
            send_sem=bx_send.at[n],
            recv_sem=bx_recv.at[n],
            device_id=dev(me - RING * to),
            device_id_type=MESH,
        )
        copy.start()
        x_backs.append(copy)

    def merge(n):
        src, q, nq, dst, to = HALO[n]
        x_backs[n].wait_recv()
        mine = frame[src : src + 32, q : q + nq].astype(F32)
        frame[src : src + 32, q : q + nq] = (mine + backs[n][...].astype(F32)).astype(BF)

    def quarters(octet):
        unit = octet // 4 if isinstance(octet, int) else lax.div(octet, 4)
        half = (unit + 1) // 3 if isinstance(octet, int) else lax.div(unit + 1, 3)
        late = (unit + 2) // 3 if isinstance(octet, int) else lax.div(unit + 2, 3)
        return ((2 - unit, 2),), ((2 * half, 1), (1 + 2 * late, 1))

    def home_part(octet, n, which):
        q, nq = quarters(octet)[which][n]
        return frame.at[pl.ds(LEFT + 8 * octet, 8), pl.ds(q, nq)]

    def send_home(octets, which):
        for octet in octets:
            yp, j = octet // 3, octet % 3
            for n, (q, nq) in enumerate(quarters(octet)[which]):
                src = home_part(octet, n, which)
                dst = y_in.at[pl.ds(8 * j, 8), pl.ds(q, nq), :, lanes]
                kind = which + n

                @pl.when(y != yp)
                def _():
                    pltpu.make_async_remote_copy(
                        src_ref=src,
                        dst_ref=dst,
                        send_sem=by_send.at[octet, kind],
                        recv_sem=by_recv.at[y, j, kind],
                        device_id=dev(base + yp),
                        device_id_type=MESH,
                    ).start()

                @pl.when(y == yp)
                def _():
                    pltpu.make_async_copy(src, dst, by_recv.at[y, j, kind]).start()

    halo_back(0)
    halo_back(1)
    pairs(out_of_slots, 5, 3, 3)
    send_home(range(0, 6), 0)
    halo_back(2)
    halo_back(3)
    pairs(out_of_slots, 8, 3, 3)
    send_home(range(6, 12), 0)
    merge(0)
    send_home(range(0, 4), 1)
    merge(1)
    send_home(range(8, 12), 1)
    merge(2)
    merge(3)
    send_home(range(4, 8), 1)

    for copy in v_copies:
        if copy is v_copies[2]:
            copy.wait()
        else:
            copy.wait_recv()
    for k in range(7):
        pot_rows[BOX * k : BOX * k + BOX, :] = v_win[k].astype(F32)[0:BOX]
    pot_rows[7 * BOX : 128, :] = jnp.zeros((128 - 7 * BOX, 1024), F32)

    near_rows = pot_rows[...].astype(BF)
    row_of = lax.broadcasted_iota(jnp.int32, (128, FRAME), 0)
    for j in range(3):
        select = (row_of == starts[pl.ds(LEFT // 8 + 3 * y + j, 1), :]).astype(F32).astype(BF)
        local = lax.dot_general(select, near_rows, (((0,), (0,)), ((), ())), preferred_element_type=F32)
        pot_own[8 * j : 8 * j + 8] = local.reshape(8, 4, 8, 1024)

    loads[2].wait()
    for which in range(2):
        for k in (0, 1, 3, 2):
            ys = lax.rem(y + k, RING)
            cols = pl.ds(pl.multiple_of(ys * SLICE, SLICE), SLICE)
            for j in range(3):
                for n, (q, nq) in enumerate(quarters(3 * y + j)[which]):
                    part = y_in.at[pl.ds(8 * j, 8), pl.ds(q, nq), :, cols]
                    pltpu.make_async_copy(part, part, by_recv.at[ys, j, which + n]).wait()
            held, local = [], []
            for j in range(3):
                for n, (q, nq) in enumerate(quarters(3 * y + j)[which]):
                    part = (slice(8 * j, 8 * j + 8), pl.ds(q, nq), slice(None), cols)
                    held.append(y_in[part].astype(F32).reshape(64 * nq, SLICE))
                    local.append(pot_own[part].reshape(64 * nq, SLICE))
            held = jnp.concatenate(held, axis=0)
            local = jnp.concatenate(local, axis=0)
            applied = jnp.dot(held.astype(BF), kin[cols, :], preferred_element_type=F32)
            if k == 0:
                x_in[...] = applied
            else:
                x_in[...] += applied
            x_in[:, cols] += local * held
        at = 0
        for j in range(3):
            for n, (q, nq) in enumerate(quarters(3 * y + j)[which]):
                piece = x_in[at : at + 64 * nq, :].astype(BF).astype(F32)
                y_res[8 * j : 8 * j + 8, pl.ds(q, nq)] = piece.reshape(8, nq, 8, 1024).astype(BF)
                at += 64 * nq

    for copy in started:
        copy.wait_send()
    for k, copy in enumerate(v_copies):
        if k != 2:
            copy.wait_send()
    for copy in s_copies:
        copy.wait_send()
    for copy in own_rows:
        copy.wait_send()

    @pl.when(y <= 2)
    def _():
        for yp in range(RING):
            pltpu.make_async_copy(rows_out.at[0], rows_out.at[0], c_send.at[3 + yp]).wait()

    @pl.when(y >= 1)
    def _():
        for yp in range(RING):
            pltpu.make_async_copy(rows_out.at[2], rows_out.at[2], c_send.at[7 + yp]).wait()

    for copy in x_backs:
        copy.wait_send()
    for octet in range(12):
        for which in range(2):
            for n in range(which + 1):
                part = home_part(octet, n, which)

                @pl.when(y != octet // 3)
                def _():
                    pltpu.make_async_copy(part, part, by_send.at[octet, which + n]).wait()


def write_kernel(pieces, rows, pieces_out, rows_out, sem):
    copies = [
        pltpu.make_async_copy(pieces, pieces_out, sem.at[0]),
        pltpu.make_async_copy(rows, rows_out, sem.at[1]),
    ]
    for copy in copies:
        copy.start()
    for copy in copies:
        copy.wait()


def on_device(coeffs, centers, kinetic, potential):
    hbm = pl.BlockSpec(memory_space=pl.ANY)
    vmem = pl.BlockSpec(memory_space=pltpu.VMEM)
    dma = pltpu.SemaphoreType.DMA
    results = pl.pallas_call(
        exchange_kernel,
        out_shape=(
            pltpu.VMEM((FUN, 4, 8, 1024), BF),
            pltpu.VMEM((FUN, FRAME), F32),
        ),
        in_specs=[hbm, hbm, hbm, hbm],
        out_specs=(vmem, vmem),
        scratch_shapes=[
            pltpu.VMEM((FRAME, 4, 8, SLICE), BF),
            pltpu.VMEM((SUP, FRAME, SLICE), BF),
            pltpu.VMEM((FRAME // 8, 8, FRAME), BF),
            pltpu.VMEM((32, 2, 8, SLICE), BF),
            pltpu.VMEM((32, 2, 8, SLICE), BF),
            pltpu.VMEM((32, 1, 8, SLICE), BF),
            pltpu.VMEM((32, 1, 8, SLICE), BF),
            pltpu.VMEM((FRAME, FRAME), F32),
            pltpu.VMEM((12, FUN // 8, 8, FRAME), BF),
            pltpu.VMEM((3, FUN, FRAME), F32),
            pltpu.VMEM((3, FUN, FRAME), BF),
            pltpu.VMEM((12, FUN, FRAME), BF),
            pltpu.VMEM((FRAME, FRAME), F32),
            pltpu.VMEM((16, 1024), BF),
            pltpu.VMEM((FRAME, 128), jnp.int32),
            pltpu.VMEM((BOX, 1024), F32),
            pltpu.VMEM((FUN, 128), jnp.int32),
            pltpu.VMEM((64, FRAME), jnp.int32),
            pltpu.VMEM((32, FRAME), jnp.int32),
            pltpu.VMEM((1024, 1024), BF),
            pltpu.VMEM((7, 16, 1024), BF),
            pltpu.VMEM((128, 1024), F32),
            pltpu.VMEM((FUN, 4, 8, 1024), F32),
            pltpu.VMEM((FUN, 4, 8, 1024), BF),
            pltpu.VMEM((384, 1024), F32),
            dma((3, 4)), dma((4, 4)), dma((10,)), dma((10,)), dma((7,)), dma((7,)),
            dma((9,)), dma((12,)), dma((11,)), dma((12,)), dma((4,)), dma((4,)),
            dma((12, 3)), dma((4, 3, 3)), dma((3,)),
        ],
        compiler_params=pltpu.CompilerParams(collective_id=0, has_side_effects=True),
        name="exchange",
    )(coeffs.reshape(FUN, 4, 8, 1024), kinetic, potential, centers.reshape(FUN, 128))
    filtered, gram_band = pl.pallas_call(
        write_kernel,
        out_shape=(
            jax.ShapeDtypeStruct((FUN, 4, 8, 1024), BF),
            jax.ShapeDtypeStruct((FUN, FRAME), F32),
        ),
        in_specs=[vmem, vmem],
        out_specs=(hbm, hbm),
        scratch_shapes=[dma((2,))],
        name="write",
    )(*[pltpu.with_memory_space_constraint(r, pltpu.VMEM) for r in results])
    return filtered.reshape(FUN, SUP, 1024), gram_band


def solution(mesh):
    placed = (P(("func", "box"), None, None), P(), P(), P(("func", "box"), None))
    return jax.shard_map(
        on_device,
        mesh=mesh,
        in_specs=placed,
        out_specs=(P(("func", "box"), None, None), P(("func", "box"), None)),
        check_vma=False,
    )
```
